32 devices in a mesh: grp: 2 (over x), slab: 16 (over z, y, core).
Axes of the slice: x: 2, y: 2, z: 4, core: 2. Of those that a mesh axis runs over, the one named last changes fastest.
Arguments:
- estimate: float32 [2, 8, 4, 48, 32], P(None, None, 'grp', 'slab'), parts along dimension 2, may hold values from -6 to 6
- measured: float32 [2, 8, 4, 48, 32], P(None, None, 'grp', 'slab'), parts along dimension 2, may hold values from -6 to 6
- sampled_lines: int32 [4, 12], P('grp'), parts along dimension 0, may hold values from 0 to 47, as said below
Outputs:
- updated: float32 [2, 8, 4, 48, 32], P(None, None, 'grp', 'slab'), parts along dimension 2
The draws below stay inside these ranges and needn't reach their ends.
There are 2 independent parts, one for each index of `grp`. The reference program is written for one: setup_inputs(seed, part) draws one part's arguments, and reference() takes and returns one part's arrays. A program takes and returns all parts, laid end to end along the dimension named above; each array names one. Nothing has to cross between parts.
Inputs may be any that keep to these rules, and one draw needn't show every extreme that they name: `sampled_lines`: lines within a frame are distinct, and every frame contains line 48 // 2.
All inputs are finite; a program needn't handle non-finite values.
Results may differ from the reference program's by a relative error of at most 0.0001.
Values sent between devices are 32-bit elements; how exact they have to be, the bound alone decides.
A program may use at most 64 MiB of HBM per device.

```python
import jax
import jax.numpy as jnp
from jax import lax

C = 8
T_SIZE = 2
KXW = 32
KY_DEV = 3
KY = 48
NS = 12
N_SLAB = 16


def draw_sampled_lines(key, part):
    frames = jnp.arange(T_SIZE, dtype=jnp.int32)

    def one_frame(frame):
        order = jax.random.permutation(jax.random.fold_in(key, frame), KY).astype(jnp.int32)
        centre = KY // 2
        where = jnp.argmax(order == centre)
        order = order.at[where].set(order[0]).at[0].set(centre)
        return order[:NS]
    return jax.vmap(one_frame)(frames).astype(jnp.int32)


def block_scale(stream_key, dims, cuts, smallest, high):
    def one(dim, parts):
        heights = jax.random.uniform(jax.random.fold_in(jax.random.fold_in(stream_key, 6), dim), (parts,), jnp.float32, smallest / len(cuts), high / len(cuts))
        return jnp.repeat(jnp.exp(heights), dims[dim] // parts).reshape((-1,) + (1,) * (len(dims) - dim - 1))

    gain = one(*cuts[0])
    for cut in cuts[1:]:
        gain = gain * one(*cut)
    return gain


def gaussian(rng, dims, spread, reach, cuts=(), held_as=jnp.bfloat16):
    drawn = jax.random.normal(rng, dims, jnp.float32) * spread
    if len(cuts) > 0:
        drawn = block_scale(rng, dims, cuts, -0.22, 0.18) * drawn
    return jnp.clip(drawn, min=-reach, max=reach).astype(held_as)


def setup_inputs(seed: int = 0, part: int = 0) -> dict:
    streams_of = jax.random.split(jax.random.key(seed), 4)
    part_splits = jax.random.split(jax.random.fold_in(streams_of[3], part), 4)
    return {
        "estimate": gaussian(part_splits[0], (2, C, T_SIZE, KY, KXW), 1.0, 6.0, ((3, 16),), jnp.float32),
        "measured": gaussian(part_splits[1], (2, C, T_SIZE, KY, KXW), 1.0, 6.0, ((3, 16),), jnp.float32),
        "sampled_lines": draw_sampled_lines(jax.random.fold_in(jax.random.fold_in(streams_of[3], part), 71), part),
    }


HIGH = lax.Precision.HIGHEST


def build_rows(ext, rows):
    pieces = []
    for shift_t in range(5):
        for shift_y in range(5):
            for shift_x in range(5):
                pieces.append(ext[:, :, shift_t:shift_t + T_SIZE, shift_y:shift_y + rows, shift_x:shift_x + KXW])
    stacked = jnp.stack(pieces, axis=-1)
    stacked = jnp.transpose(stacked, (0, 2, 3, 4, 1, 5))
    return stacked.reshape(2, T_SIZE * rows * KXW, C * 125)


def fold_rows(filtered, rows):
    shaped = filtered.reshape(2, T_SIZE, rows, KXW, C, 125)
    shaped = jnp.transpose(shaped, (0, 4, 1, 2, 3, 5))
    result = jnp.zeros((2, C, T_SIZE + 4, rows + 4, KXW + 4), jnp.float32)
    offset = 0
    for shift_t in range(5):
        for shift_y in range(5):
            for shift_x in range(5):
                result = result.at[:, :, shift_t:shift_t + T_SIZE, shift_y:shift_y + rows, shift_x:shift_x + KXW].add(shaped[..., offset])
                offset += 1
    return result / 125.0


def reference(estimate, measured, sampled_lines):
    padded = jnp.pad(estimate, ((0, 0), (0, 0), (2, 2), (2, 2), (2, 2)))
    width = 125 * C
    starts = jnp.arange(N_SLAB, dtype=jnp.int32) * KY_DEV

    def gram_step(carry, start):
        ext = lax.dynamic_slice_in_dim(padded, start, KY_DEV + 4, 3)
        patch = build_rows(ext, KY_DEV)
        real_part, imag_part = patch[0], patch[1]
        real_gram = jnp.dot(real_part.T, real_part, precision=HIGH) + jnp.dot(imag_part.T, imag_part, precision=HIGH)
        imag_gram = jnp.dot(real_part.T, imag_part, precision=HIGH) - jnp.dot(imag_part.T, real_part, precision=HIGH)
        return (carry[0] + real_gram, carry[1] + imag_gram), None

    zeros = jnp.zeros((width, width), jnp.float32)
    (real_gram, imag_gram), unused = lax.scan(gram_step, (zeros, zeros), starts)
    scale = jnp.trace(real_gram) / width + 1e-6
    real_gram = real_gram / scale
    imag_gram = imag_gram / scale

    def fold_step(total, start):
        ext = lax.dynamic_slice_in_dim(padded, start, KY_DEV + 4, 3)
        patch = build_rows(ext, KY_DEV)
        real_part, imag_part = patch[0], patch[1]
        real_out = jnp.dot(real_part, real_gram, precision=HIGH) - jnp.dot(imag_part, imag_gram, precision=HIGH)
        imag_out = jnp.dot(real_part, imag_gram, precision=HIGH) + jnp.dot(imag_part, real_gram, precision=HIGH)
        piece = fold_rows(jnp.stack([real_out, imag_out]), KY_DEV)
        current = lax.dynamic_slice_in_dim(total, start, KY_DEV + 4, 3)
        total = lax.dynamic_update_slice_in_dim(total, current + piece, start, 3)
        return total, None

    total = jnp.zeros((2, C, T_SIZE + 4, KY + 4, KXW + 4), jnp.float32)
    total, unused = lax.scan(fold_step, total, starts)
    folded = total[:, :, 2:-2, 2:-2, 2:-2]
    rows = jnp.arange(KY, dtype=jnp.int32)
    hit = jnp.any(sampled_lines[:, :, None] == rows[None, None, :], axis=1)
    weight = hit.astype(jnp.float32)[None, None, :, :, None]
    return weight * measured + (1.0 - weight) * folded
```

```python
import functools

import jax
import jax.numpy as jnp
from jax import lax
from jax.experimental import pallas as pl
from jax.experimental.pallas import tpu as pltpu
from jax.sharding import PartitionSpec as P

LANES = 128
REACH = 4
CHUNK = 24


def couplings(frames):
    table = {}
    for s in range(frames):
        for s2 in range(frames):
            for d in range(1 - frames, frames):
                if 0 <= s + d < frames and 0 <= s2 + d < frames:
                    table[s, s2, d] = sum(
                        1
                        for t in range(frames)
                        if 0 <= t + d < frames and abs(s - t) <= 2 and abs(s2 - t) <= 2
                    )
    return {k: v for k, v in table.items() if v}


def split(x):
    hi = x.astype(jnp.bfloat16).astype(jnp.float32)
    return hi, x - hi


def dot_nt(a, b):
    return lax.dot_general(a, b, (((1,), (1,)), ((), ())), preferred_element_type=jnp.float32)


def dot_nn(a, b):
    return lax.dot_general(a, b, (((1,), (0,)), ((), ())), preferred_element_type=jnp.float32)


def as_bf16(pieces):
    return jnp.concatenate(pieces, axis=0).astype(jnp.bfloat16)


def kernel(
    n, sizes, est_hbm, meas_hbm, picks_hbm, out_ref,
    est, meas, picks, all_ref, left, r_hi, r_lo, weights, p_hi, p_lo, sums, edges,
    send_sem, recv_sem, in_sem,
):
    parts, frames, coils, rows, readout = sizes
    me = lax.axis_index("slab")
    total = n * rows
    deep = total // 2
    chunk = max(d for d in range(1, CHUNK + 1) if deep % d == 0)
    ext = coils * 5
    wide = frames * ext

    loads = [
        pltpu.make_async_copy(est_hbm, est, in_sem.at[0]),
        pltpu.make_async_copy(meas_hbm, meas, in_sem.at[1]),
        pltpu.make_async_copy(picks_hbm, picks, in_sem.at[2]),
    ]
    for copy in loads:
        copy.start()

    def greet(k, carry):
        pl.semaphore_signal(
            pltpu.get_barrier_semaphore(), inc=1, device_id={"slab": lax.rem(me + k, n)}
        )
        return carry

    lax.fori_loop(1, n, greet, 0, unroll=n <= 16)

    def place(line, s, part):
        return pl.ds((part * coils * rows + line) * frames + s, coils, stride=rows * frames)

    loads[0].wait()
    for j in range(rows):
        all_ref[me, j * coils : (j + 1) * coils, :] = jnp.concatenate(
            [est[place(j, s, part), :] for part in range(parts) for s in range(frames)], axis=1
        )
    pl.semaphore_wait(pltpu.get_barrier_semaphore(), n - 1)

    def copy(other, slot):
        return pltpu.make_async_remote_copy(
            src_ref=all_ref.at[slot],
            dst_ref=all_ref.at[slot],
            send_sem=send_sem.at[other],
            recv_sem=recv_sem.at[slot],
            device_id={"slab": other},
        )

    def send(k, carry):
        copy(k + (k >= me).astype(jnp.int32), me).start()
        return carry

    lax.fori_loop(0, n - 1, send, 0, unroll=n <= 16)

    lane = lax.broadcasted_iota(jnp.int32, (1, LANES), 1)
    slot = lane // readout
    x = lane % readout
    second = slot % 2 == 1
    turn = jnp.where(slot < 2, 1.0, -1.0)

    def rolled(v, by):
        by = by % LANES
        return pltpu.roll(v, by, 1) if by else v

    def shifts(v):
        return [
            jnp.where((x + d >= 0) & (x + d < readout), rolled(v, -d), 0.0) if d else v
            for d in range(-2, 3)
        ]

    def halo(d):
        return (me + d >= 0) & (me + d < n)

    near = -(-REACH // rows)
    for d in [s * k for k in range(1, near + 1) for s in (1, -1)]:
        pl.when(halo(d))(lambda d=d: copy(me + d, me + d).wait_recv())

    around = []
    for i in range(rows + 2 * REACH):
        d, j = divmod(i - REACH, rows)
        block = all_ref[jnp.clip(me + d, 0, n - 1), j * coils : (j + 1) * coils, :]
        block = jnp.where(halo(d), block, 0.0) if d else block
        around.append([rolled(block, by * readout) for by in range(LANES // readout)])

    moved = {}
    for dy in range(-REACH, REACH + 1):
        for s in range(frames):
            for part in range(parts):
                v = jnp.zeros((coils, LANES), jnp.float32)
                for j in range(rows):
                    seg = part * frames + s
                    v = jnp.where(slot == j, around[dy + REACH + j][(j - seg) % 4], v)
                moved[dy, s, part] = shifts(v)

    line_at = me * rows + slot

    def coefficient(dy, q=None):
        count = jnp.zeros((1, LANES), jnp.float32)
        for b in range(max(-2, -2 - dy), min(2, 2 - dy) + 1):
            if q is not None and 0 <= q - b < total:
                continue
            count = count + jnp.where((line_at - b >= 0) & (line_at - b < total), 1.0, 0.0)
        return count if q is None else -count

    blocks = [[(dy, None) for dy in range(first, first + 3)] for first in (-4, -1, 2)]
    ends = [
        (0, 0, False, 0, [(0, 0), (1, 0), None]),
        (1, 0, False, 0, [(-1, 1), (0, 1), None]),
        (deep - 1, deep - 2, True, total - 1, [(-1, total - 1), (0, total - 1), None]),
        (deep - 2, deep - 2, True, total - 2, [(0, total - 2), (1, total - 2), None]),
    ]
    blocks += [e[4] for e in ends]
    nothing = jnp.zeros((coils, LANES), jnp.float32)
    tile = frames * LANES
    for t, members in enumerate(blocks):
        for s in range(frames):
            his, los = [[], []], [[], []]
            for member in members:
                factor = None if member is None else coefficient(*member)
                for e in range(5):
                    for part in range(parts):
                        if member is None:
                            hi = lo = nothing
                        else:
                            hi, lo = split(factor * moved[member[0], s, part][e])
                        his[part].append(hi)
                        los[part].append(lo)
            for part in range(parts):
                his[part].append(nothing)
                los[part].append(nothing)
            at = pl.ds(t * tile + s * LANES, LANES)
            bt = pl.ds((len(blocks) + t) * tile + s * LANES, LANES)
            for ref, cells in ((p_hi, his), (p_lo, los)):
                re, im = as_bf16(cells[0]), as_bf16(cells[1])
                ref[at, 0:LANES] = re
                ref[at, LANES : 2 * LANES] = im
                ref[bt, 0:LANES] = -im
                ref[bt, LANES : 2 * LANES] = re

    def arrive(j, carry):
        pl.when(jnp.abs(j - me) > near)(lambda: copy(j, j).wait_recv())
        return carry

    lax.fori_loop(0, n, arrive, 0, unroll=n <= 16)

    def line_block(line):
        if isinstance(line, int):
            if not 0 <= line < total:
                return None
            return all_ref[line // rows, line % rows * coils : (line % rows + 1) * coils, :]
        inside = jnp.clip(line, 0, total - 1)
        block = all_ref[inside // rows, pl.ds(pl.multiple_of(inside % rows * coils, coils), coils), :]
        return jnp.where((line >= 0) & (line < total), block, 0.0)

    def reach_of(line):
        return sum(
            ((line - b >= 0) & (line - b < total)) * jnp.float32(1) for b in range(-2, 3)
        )

    def build(first, energy):
        tiles = {}
        for k in range(-REACH, chunk + REACH):
            lines = [line_block(first + k), line_block(first + k + deep)]
            if 0 <= k < chunk:
                for h in range(2):
                    energy = energy + reach_of(first + k + deep * h) * (lines[h] * lines[h])
            lines = [nothing if v is None else v for v in lines]
            cells = []
            for s in range(frames):
                v = jnp.where(
                    second,
                    rolled(lines[1], (1 - s) * readout),
                    rolled(lines[0], -s * readout),
                )
                cells.append(shifts(v))
            tiles[k] = [[split(v) for v in c] for c in cells]
            if 0 <= k < chunk:
                flat = [p for c in tiles[k] for p in c]
                at = pl.ds(k * LANES, LANES)
                for w in range(2):
                    left[pl.ds(w * 2 * wide, wide), at] = as_bf16([p[w] for p in flat])
                    left[pl.ds(w * 2 * wide + wide, wide), at] = as_bf16(
                        [turn * rolled(p[w], LANES // 2) for p in flat]
                    )
            if k - 2 >= -REACH:
                at = pl.ds((k - 2 + REACH) * LANES, LANES)
                for s in range(frames):
                    for ref, w in ((r_hi, 0), (r_lo, 1)):
                        ref[pl.ds(s * LANES, LANES), at] = as_bf16(
                            [p[w] for m in (k - 2, k - 1, k) for p in tiles[m][s]] + [nothing]
                        )
        return energy

    def product(rows_, right):
        both = dot_nt(rows_, r_hi[:, right])
        rest = dot_nt(rows_[: 2 * wide], r_lo[:, right])
        return both[: 2 * wide] + both[2 * wide :] + rest

    def gram(first):
        return product(left[...], pl.ds((first + REACH) * LANES, chunk * LANES))

    def end(which, base):
        at, start, late, _, _ = ends[which]
        rows_ = left[:, pl.ds((at - base) * LANES, LANES)]
        rows_ = jnp.where(second == late, rows_, jnp.zeros_like(rows_))
        return product(rows_, pl.ds((start - base + REACH) * LANES, LANES))

    energy = nothing
    if chunk == deep:
        energy = build(0, energy)
        found = [gram(m[0][0]) for m in blocks[:3]] + [end(w, 0) for w in range(4)]
    else:
        for t in range(3):
            sums[t] = jnp.zeros((2 * wide, tile), jnp.float32)

        def step(c, energy):
            energy = build(c * chunk, energy)
            for t in range(3):
                sums[t] += gram(blocks[t][0][0])

            @pl.when(c == 0)
            def _():
                for w in range(2):
                    edges[w] = end(w, 0)

            @pl.when(c == deep // chunk - 1)
            def _():
                for w in range(2, 4):
                    edges[w] = end(w, deep - chunk)

            return energy

        energy = lax.fori_loop(0, deep // chunk, step, energy)
        found = [sums[t] for t in range(3)] + [edges[w] for w in range(4)]

    across = sum(jnp.where((x - d >= 0) & (x - d < readout), 1.0, 0.0) for d in range(-2, 3))
    frame = slot % frames
    for s in range(frames):
        reach = sum(1.0 for t in range(frames) if abs(s - t) <= 2)
        across = jnp.where(frame == s, across * reach, across)
    energy = jnp.sum(energy * across, axis=0, keepdims=True)
    scale = jnp.sum(energy, axis=1, keepdims=True) / (125 * coils) + 1e-06

    table = couplings(frames)
    for t, u in enumerate(found):
        for h in range(2):
            for s in range(frames):
                pieces = []
                for s2 in range(frames):
                    total_ = None
                    for d in range(1 - frames, frames):
                        if (s2, s, d) in table:
                            row = h * wide + (s2 + d) * ext
                            term = u[row : row + ext, (s + d) * LANES : (s + d + 1) * LANES]
                            term = float(table[s2, s, d]) * term
                            total_ = term if total_ is None else total_ + term
                    pieces.append(total_)
                hi, lo = split(jnp.concatenate(pieces, axis=0))
                at = pl.ds((h * len(blocks) + t) * tile + s * LANES, LANES)
                weights[0:wide, at] = hi.astype(jnp.bfloat16)
                weights[wide : 2 * wide, at] = lo.astype(jnp.bfloat16)

    both = dot_nn(weights[...], p_hi[...])
    y = both[:wide] + both[wide:] + dot_nn(weights[0:wide, :], p_lo[...])

    factor = 1.0 / (125.0 * scale)
    for copy_ in loads[1:]:
        copy_.wait()
    chosen = picks[...]
    for s in range(frames):
        for part in range(parts):
            folded = jnp.zeros((coils, LANES), jnp.float32)
            for e in range(5):
                v = y[(s * 5 + e) * coils : (s * 5 + e + 1) * coils, part * LANES : (part + 1) * LANES]
                d = e - 2
                v = jnp.where((x - d >= 0) & (x - d < readout), rolled(v, d), 0.0) if d else v
                folded = folded + v
            folded = folded * factor
            for j in range(rows):
                hit = jnp.where(chosen[s : s + 1, :] == me * rows + j, 1.0, 0.0)
                hit = jnp.max(hit, axis=1, keepdims=True)
                at = place(j, s, part)
                out_ref[at, :] = jnp.where(
                    hit > 0.5, meas[at, :], rolled(folded, -j * readout)[:, :readout]
                )

    def finish(k, carry):
        copy(k + (k >= me).astype(jnp.int32), me).wait_send()
        return carry

    lax.fori_loop(0, n - 1, finish, 0)


def local(estimate, measured, sampled_lines):
    parts, coils, frames, rows, readout = estimate.shape
    n = lax.axis_size("slab")
    assert parts * frames * readout == LANES and frames == 2 and coils % 8 == 0
    assert rows * readout <= LANES and n * rows % 2 == 0 and n * rows >= 16
    flat = (parts * coils * rows * frames, readout)
    deep = n * rows // 2
    chunk = max(d for d in range(1, CHUNK + 1) if deep % d == 0)
    wide = frames * 5 * coils
    tile = frames * LANES
    kinds = 7
    single = chunk == deep
    bf16 = jnp.bfloat16
    any_space = pl.BlockSpec(memory_space=pltpu.HBM)
    stay = functools.partial(pltpu.with_memory_space_constraint, memory_space=pltpu.HBM)
    out = pl.pallas_call(
        functools.partial(kernel, n, (parts, frames, coils, rows, readout)),
        out_shape=jax.ShapeDtypeStruct(flat, jnp.float32),
        in_specs=[any_space] * 3,
        out_specs=pl.BlockSpec(memory_space=pltpu.VMEM),
        scratch_shapes=[
            pltpu.VMEM(flat, jnp.float32),
            pltpu.VMEM(flat, jnp.float32),
            pltpu.VMEM(sampled_lines.shape, jnp.int32),
            pltpu.VMEM((n, rows * coils, LANES), jnp.float32),
            pltpu.VMEM((4 * wide, chunk * LANES), bf16),
            pltpu.VMEM((tile, (chunk + 6) * LANES), bf16),
            pltpu.VMEM((tile, (chunk + 6) * LANES), bf16),
            pltpu.VMEM((2 * wide, 2 * kinds * tile), bf16),
            pltpu.VMEM((2 * kinds * tile, parts * LANES), bf16),
            pltpu.VMEM((2 * kinds * tile, parts * LANES), bf16),
            pltpu.VMEM((1 if single else 3, 2 * wide, tile), jnp.float32),
            pltpu.VMEM((1 if single else 4, 2 * wide, tile), jnp.float32),
            pltpu.SemaphoreType.DMA((n,)),
            pltpu.SemaphoreType.DMA((n,)),
            pltpu.SemaphoreType.DMA((3,)),
        ],
        compiler_params=pltpu.CompilerParams(
            vmem_limit_bytes=40 * 1024 * 1024, collective_id=0, has_side_effects=True
        ),
    )(
        stay(jnp.transpose(estimate, (0, 1, 3, 2, 4)).reshape(flat)),
        stay(jnp.transpose(measured, (0, 1, 3, 2, 4)).reshape(flat)),
        stay(sampled_lines),
    )
    return jnp.transpose(out.reshape(parts, coils, rows, frames, readout), (0, 1, 3, 2, 4))


def solution(mesh):
    placed = (
        P(None, None, "grp", "slab", None),
        P(None, None, "grp", "slab", None),
        P("grp", None),
    )
    return jax.shard_map(
        local,
        mesh=mesh,
        in_specs=placed,
        out_specs=P(None, None, "grp", "slab", None),
        check_vma=False,
    )
```

```python
import functools

import jax
import jax.numpy as jnp
from jax import lax
from jax.experimental import pallas as pl
from jax.experimental.pallas import tpu as pltpu
from jax.sharding import PartitionSpec as P

LANES = 128
REACH = 4
SPAN = range(-REACH, REACH + 1)
SMALL = 16


def couplings(frames):
    table = {}
    for s in range(frames):
        for s2 in range(frames):
            for d in range(1 - frames, frames):
                if 0 <= s + d < frames and 0 <= s2 + d < frames:
                    table[s, s2, d] = sum(
                        1
                        for t in range(frames)
                        if 0 <= t + d < frames and abs(s - t) <= 2 and abs(s2 - t) <= 2
                    )
    return {k: v for k, v in table.items() if v}


def halves(x):
    hi = x.astype(jnp.bfloat16)
    return hi, (x - hi.astype(jnp.float32)).astype(jnp.bfloat16)


def dot_nt(a, b):
    return lax.dot_general(a, b, (((1,), (1,)), ((), ())), preferred_element_type=jnp.float32)


def dot_nn(a, b):
    return lax.dot_general(a, b, (((1,), (0,)), ((), ())), preferred_element_type=jnp.float32)


def kernel(
    n, sizes, est_hbm, meas_hbm, picks_hbm, out_ref,
    est, meas, picks, all_ref, even, odd, base, sums, shift, flat, patch, u_hi, u_lo,
    send_sem, recv_sem, in_sem, ready,
):
    parts, frames, coils, rows, readout = sizes
    me = lax.axis_index("slab")
    flip = me >= n - 4
    mine = jnp.where(flip, n - 1 - me, me)
    total = n * rows
    ext = coils * 5
    wide = frames * ext
    bf16 = jnp.bfloat16

    loads = [
        pltpu.make_async_copy(est_hbm, est, in_sem.at[0]),
        pltpu.make_async_copy(meas_hbm, meas, in_sem.at[1]),
        pltpu.make_async_copy(picks_hbm, picks, in_sem.at[2]),
    ]
    for load in loads:
        load.start()

    def greet(j, carry):
        pl.semaphore_signal(pltpu.get_barrier_semaphore(), inc=1, device_id={"slab": j})
        return carry

    lax.fori_loop(me + 1, n, greet, 0)

    def place(line, s, part):
        return pl.ds((part * coils * rows + line) * frames + s, coils, stride=rows * frames)

    loads[0].wait()
    for j in range(rows):
        all_ref[me, j * coils : (j + 1) * coils, :] = jnp.concatenate(
            [est[place(j, s, part), :] for part in range(parts) for s in range(frames)], axis=1
        )
    pl.when(me > 0)(lambda: pl.semaphore_wait(pltpu.get_barrier_semaphore(), me))

    def copy(other, slot):
        return pltpu.make_async_remote_copy(
            src_ref=all_ref.at[slot],
            dst_ref=all_ref.at[slot],
            send_sem=send_sem.at[other],
            recv_sem=recv_sem.at[slot],
            device_id={"slab": other},
        )

    def down(j, carry):
        pl.semaphore_signal(ready.at[me], inc=1, device_id={"slab": j})
        copy(j, me).start()
        return carry

    lax.fori_loop(0, me, down, 0)

    def meet(j, carry):
        pl.semaphore_wait(ready.at[j], 1)
        copy(j, me).start()
        return carry

    first_group = me < 4

    def meet_group(t):
        stop = jnp.where(first_group, 4 * t + 4, me + 1)
        lax.fori_loop(jnp.where(first_group, jnp.maximum(me + 1, 4 * t), me + 1), stop, meet, 0)

    lax.fori_loop(me + 1, jnp.where(first_group, me + 1, n), meet, 0)
    meet_group(0)
    meet_group(1)

    def take(k):
        j = jnp.where(flip, n - 1 - k, k)
        pl.when(j != me)(lambda: copy(j, j).wait_recv())

    lane = lax.broadcasted_iota(jnp.int32, (1, LANES), 1)
    slot = lane // readout
    x = lane % readout
    second = slot >= parts
    turn = jnp.where(slot % parts == 0, 1.0, -1.0)
    nothing = jnp.zeros((coils, LANES), jnp.float32)

    def rolled(v, by):
        by = by % LANES
        return pltpu.roll(v, by, 1) if by else v

    def shifts(v):
        return [
            jnp.where((x + d >= 0) & (x + d < readout), rolled(v, -d), 0.0) if d else v
            for d in range(-2, 3)
        ]

    def line_block(line):
        if isinstance(line, int) and not 0 <= line < total:
            return nothing
        dev, j = line // rows, line % rows
        dev = jnp.where(flip, n - 1 - dev, dev)
        j = jnp.where(flip, rows - 1 - j, j)
        return all_ref[dev, pl.ds(pl.multiple_of(j * coils, coils), coils), :]

    order = [(s, e) for s in range(frames) for e in range(5)]

    def reach_of(line):
        inside = [(line - b >= 0) & (line - b < total) for b in range(-2, 3)]
        if isinstance(line, int):
            return float(sum(inside))
        return sum(jnp.where(v, 1.0, 0.0) for v in inside)

    def at_tile(i):
        start = (i // 2 + 2) * LANES
        return pl.ds(start if isinstance(i, int) else pl.multiple_of(start, LANES), LANES)

    pieces_of = len(order)
    row = lax.broadcasted_iota(jnp.int32, (LANES, LANES), 0)
    part_at = slot % parts
    for b, (s, e) in enumerate(order):
        for k, part in enumerate((part_at, 1 - part_at)):
            from_x = x + e - 2
            target = jnp.where(
                (from_x >= 0) & (from_x < readout), (part * frames + s) * readout + from_x, -1
            )
            one = 1.0 if k == 0 else turn
            shift[:, (k * pieces_of + b) * LANES : (k * pieces_of + b + 1) * LANES] = jnp.where(
                row == target, one, 0.0
            ).astype(bf16)

    def absorb(first, count, energy):
        lines = [line_block(first + k) for k in range(count + 1)]
        for k in range(1, count + 1):
            line = first + k
            if not isinstance(line, int) or line < total:
                energy = energy + reach_of(line) * (lines[k] * lines[k])
        raw = jnp.concatenate(lines, axis=0)
        high = raw.astype(bf16).astype(jnp.float32)
        split = jnp.concatenate([high, raw - high], axis=0).astype(bf16)
        g = dot_nn(split, shift[...])

        def piece(k, w, b):
            top = (w * (count + 1) + k) * coils
            return g[top : top + coils, b * LANES : (b + 1) * LANES]

        for step in range(count):
            i = first + step
            is_even = (step + PARITY) % 2 == 0
            tiles = even if is_even else odd
            at = at_tile(i)
            for w in range(2):
                cells = [
                    jnp.where(second, piece(step + 1, w, b), piece(step, w, b))
                    for b in range(pieces_of)
                ]
                tiles[w * wide : (w + 1) * wide, at] = jnp.concatenate(cells, axis=0).astype(bf16)
                if is_even and (not isinstance(i, int) or 0 <= i < total):
                    both = [
                        jnp.where(second, piece(step + 1, w, b), piece(step, w, b))
                        for b in range(pieces_of, 2 * pieces_of)
                    ]
                    stacked = []
                    for s in range(frames):
                        stacked += [cells[order.index((s, e))] for e in range(5)]
                        stacked += [both[order.index((s, e))] for e in range(5)]
                    base[w * 2 * wide : (w + 1) * 2 * wide, at] = jnp.concatenate(
                        stacked, axis=0
                    ).astype(bf16)
        return energy

    gap = jnp.zeros((LANES - 2 * ext, 1), bf16)

    def columns(at, w, count):
        pad = jnp.broadcast_to(gap, (LANES - 2 * ext, count * LANES))
        pieces = []
        for s in range(frames):
            top = w * 2 * wide + s * 2 * ext
            pieces += [base[top : top + 2 * ext, at], pad]
        return jnp.concatenate(pieces, axis=0)

    def lanes_from(tile, count):
        start = (tile + 2) * LANES
        return pl.ds(start if isinstance(tile, int) else pl.multiple_of(start, LANES), count * LANES)

    def stretch(i, w, count):
        tiles = even if i % 2 == 0 else odd
        return tiles[w * wide : (w + 1) * wide, lanes_from(i // 2, count)]

    def product(rows_hi, rows_lo, cols_hi, cols_lo):
        return dot_nt(
            jnp.concatenate([rows_hi, rows_lo, rows_hi], axis=1),
            jnp.concatenate([cols_hi, cols_hi, cols_lo], axis=1),
        )

    def gram(tile, count, fresh=False):
        at = lanes_from(tile, count)

        def moved(w):
            pieces = []
            for dy in range(REACH + 1):
                tiles = even if dy % 2 == 0 else odd
                pieces.append(tiles[w * wide : (w + 1) * wide, lanes_from(tile + dy // 2, count)])
            return jnp.concatenate(pieces, axis=0)

        g = product(moved(0), moved(1), columns(at, 0, count), columns(at, 1, count))
        sums[...] = g if fresh else sums[...] + g

    def edge(i):
        at = lanes_from(i // 2, 1)

        def picked(w):
            zero = jnp.zeros((wide, LANES), bf16)
            return jnp.concatenate(
                [
                    jnp.where(second, zero, stretch(i, w, 1)),
                    jnp.where(second, zero, stretch(i + 1, w, 1)),
                    jnp.where(second, stretch(i - 1, w, 1), zero),
                    jnp.where(second, stretch(i, w, 1), zero),
                ],
                axis=0,
            )

        return product(picked(0), picked(1), columns(at, 0, 1), columns(at, 1, 1))

    ahead = REACH + 1
    members = [(dy, None) for dy in (*range(ahead), *range(-1, -ahead, -1))]
    for i in (0, total - 2):
        members += [(0, i), (1, i), (-1, i + 1), (0, i + 1)]
    depth = len(members) * wide
    deep = -(-depth // LANES) * LANES
    cells_here = rows * readout

    def patches():
        line_at = mine * rows + slot

        def coefficient(dy, q=None):
            count = jnp.zeros((1, LANES), jnp.float32)
            for b in range(max(-2, -2 - dy), min(2, 2 - dy) + 1):
                if q is not None and 0 <= q - b < total:
                    continue
                count = count + jnp.where((line_at - b >= 0) & (line_at - b < total), 1.0, 0.0)
            return count if q is None else -count

        around = []
        for i in range(rows + 2 * REACH):
            line = mine * rows - REACH + i
            block = line_block(jnp.clip(line, 0, total - 1))
            block = jnp.where((line >= 0) & (line < total), block, 0.0)
            around.append([rolled(block, by * readout) for by in range(LANES // readout)])
        for dy in SPAN:
            for part in range(parts):
                cells = []
                for s in range(frames):
                    v = nothing
                    for j in range(rows):
                        seg = part * frames + s
                        v = jnp.where(slot == j, around[dy + REACH + j][(j - seg) % 4], v)
                    cells.append(shifts(v))
                v = jnp.concatenate([cells[s][e] for s, e in order], axis=0)
                for t, (dy2, q) in enumerate(members):
                    if dy2 == dy:
                        factor = float(couplings(frames)[0, 0, 0]) * coefficient(dy, q)
                        flat[part, t * wide : (t + 1) * wide, :] = factor * v
        for part in range(parts):
            for k in range(0, deep, LANES):
                hi, lo = halves(flat[part, k : k + LANES, :].T[:cells_here])
                at = pl.ds(k, LANES)
                patch[pl.ds(part * cells_here, cells_here), at] = hi
                patch[pl.ds((parts + part) * cells_here, cells_here), at] = lo

    table = couplings(frames)
    unit = float(table[0, 0, 0])

    def mixed(u):
        result = []
        for s2 in range(frames):
            pieces = []
            for s in range(frames):
                whole = None
                for d in range(1 - frames, frames):
                    if (s, s2, d) in table:
                        row = (s + d) * ext
                        term = u[row : row + ext, (s2 + d) * LANES : (s2 + d + 1) * LANES]
                        factor = table[s, s2, d] / unit
                        term = term if factor == 1 else factor * term
                        whole = term if whole is None else whole + term
                pieces.append(whole)
            result.append(jnp.concatenate(pieces, axis=0))
        return result

    def settle(t, cells):
        for s2 in range(frames):
            hi, lo = halves(cells[s2])
            at = pl.ds(s2 * LANES, LANES)
            u_hi[t * wide : (t + 1) * wide, at] = hi
            u_lo[t * wide : (t + 1) * wide, at] = lo

    def mirrored(cells):
        pieces = [[], []]
        for s in range(frames):
            spare = jnp.zeros((LANES - wide, LANES), jnp.float32)
            v = jnp.concatenate([cells[s], spare], axis=0).T
            re, im = v[:ext], v[ext : 2 * ext]
            pieces[0].append(jnp.where(lane < ext, re, -rolled(im, ext)))
            pieces[1].append(jnp.where(lane < ext, rolled(re, -ext), -im))
        return [jnp.concatenate(p, axis=0) for p in pieces]

    for i in (total, total + 1, total + 2):
        tiles = even if i % 2 == 0 else odd
        tiles[:, at_tile(i)] = jnp.zeros((2 * wide, LANES), bf16)
    for part in range(parts):
        flat[part, depth:deep, :] = jnp.zeros((deep - depth, LANES), jnp.float32)
    for ref in (u_hi, u_lo):
        ref[depth:deep, :] = jnp.zeros((deep - depth, frames * LANES), bf16)

    group = 4 * rows
    groups = n // 4
    half = group // 2

    def settle_edge(first, i):
        g = edge(i)
        for k in range(4):
            settle(first + k, mixed(g[k * wide : (k + 1) * wide]))

    energy = nothing
    PARITY = 1
    if n <= SMALL:
        for t in range(groups):
            last = t == groups - 1
            for h in range(2):
                for k in (4 * t + 2 * h, 4 * t + 2 * h + 1):
                    take(k)
                first = group * t + half * h - 1
                PARITY = first % 2
                energy = absorb(first, half + (last and h == 1), energy)
                if last and h == 0:
                    gram((group * t - REACH) // 2, 2)
                    patches()
            lo = max(0, group * t - REACH + (REACH if last else 0))
            hi = group * t + group - (0 if last else REACH)
            if t == 1:
                lo = 0
            if t:
                gram(lo // 2, (hi - lo) // 2, fresh=t == 1)
            if t + 2 < groups:
                meet_group(t + 2)
            if t == 0:
                settle_edge(len(SPAN), 0)
    else:
        lax.fori_loop(2, groups, lambda t, c: (meet_group(t), c)[1], 0)

        def pairs(t):
            for k in range(4):
                take(4 * t + k)

        pairs(0)
        energy = absorb(-1, group, energy)
        gram(0, (group - REACH) // 2, fresh=True)
        settle_edge(len(SPAN), 0)

        def step(t, energy):
            pairs(t)
            energy = absorb(group * t - 1, group, energy)
            gram((group * t - REACH) // 2, group // 2)
            return energy

        energy = lax.fori_loop(1, groups - 1, step, energy)
        pairs(groups - 1)
        first = group * (groups - 1)
        energy = absorb(first - 1, group + 1, energy)
        gram((first - REACH) // 2, (group + REACH) // 2)
        patches()

    settle_edge(len(SPAN) + 4, total - 2)
    for t in range(ahead):
        cells = mixed(sums[t * wide : (t + 1) * wide, :])
        settle(t, cells)
        if t:
            settle(REACH + t, mirrored(cells))

    across = sum(jnp.where((x - d >= 0) & (x - d < readout), 1.0, 0.0) for d in range(-2, 3))
    frame = slot % frames
    for s in range(frames):
        reach = sum(1.0 for t in range(frames) if abs(s - t) <= 2)
        across = jnp.where(frame == s, across * reach, across)
    energy = jnp.sum(energy * across, axis=0, keepdims=True)
    scale = jnp.sum(energy, axis=1, keepdims=True) / (125 * coils) + 1e-06
    factor = 1.0 / (125.0 * scale)

    tall = parts * cells_here
    both = dot_nn(patch[...], u_hi[...])
    y = both[:tall] + both[tall:] + dot_nn(patch[0:tall, :], u_lo[...])

    for load in loads[1:]:
        load.wait()
    chosen = picks[...]
    spare = jnp.zeros((LANES - cells_here, LANES), jnp.float32)
    for s in range(frames):
        turned = []
        for part in range(parts):
            v = y[part * cells_here : (part + 1) * cells_here, s * LANES : (s + 1) * LANES]
            turned.append((jnp.concatenate([v, spare], axis=0) if cells_here < LANES else v).T)
        for part in range(parts):
            folded = nothing
            for e in range(5):
                plain = slice(e * coils, (e + 1) * coils)
                cross = slice(ext + e * coils, ext + (e + 1) * coils)
                if part == 0:
                    v = turned[0][plain] - turned[1][cross]
                else:
                    v = turned[0][cross] + turned[1][plain]
                d = e - 2
                v = jnp.where((x - d >= 0) & (x - d < readout), rolled(v, d), 0.0) if d else v
                folded = folded + v
            folded = folded * factor
            for j in range(rows):
                hit = jnp.where(chosen[s : s + 1, :] == me * rows + j, 1.0, 0.0)
                hit = jnp.max(hit, axis=1, keepdims=True)
                at = place(j, s, part)
                there = jnp.where(
                    flip, rolled(folded, (j + 1 - rows) * readout), rolled(folded, -j * readout)
                )
                out_ref[at, :] = jnp.where(hit > 0.5, meas[at, :], there[:, :readout])

    def finish(k, carry):
        copy(k + (k >= me).astype(jnp.int32), me).wait_send()
        return carry

    lax.fori_loop(0, n - 1, finish, 0)


def local(estimate, measured, sampled_lines):
    parts, coils, frames, rows, readout = estimate.shape
    n = lax.axis_size("slab")
    assert parts * frames * readout == LANES and frames == 2 and coils == 8
    assert rows * readout <= LANES and n % 4 == 0 and n >= 8 and 4 * rows >= 3 * REACH
    flat = (parts * coils * rows * frames, readout)
    total = n * rows
    wide = frames * 5 * coils
    span = (total // 2 + 4) * LANES
    deep = -(-(len(SPAN) + 8) * wide // LANES) * LANES
    cells = rows * readout
    bf16 = jnp.bfloat16
    stay = functools.partial(pltpu.with_memory_space_constraint, memory_space=pltpu.HBM)
    out = pl.pallas_call(
        functools.partial(kernel, n, (parts, frames, coils, rows, readout)),
        out_shape=jax.ShapeDtypeStruct(flat, jnp.float32),
        in_specs=[pl.BlockSpec(memory_space=pltpu.HBM)] * 3,
        out_specs=pl.BlockSpec(memory_space=pltpu.VMEM),
        scratch_shapes=[
            pltpu.VMEM(flat, jnp.float32),
            pltpu.VMEM(flat, jnp.float32),
            pltpu.VMEM(sampled_lines.shape, jnp.int32),
            pltpu.VMEM((n, rows * coils, LANES), jnp.float32),
            pltpu.VMEM((2 * wide, span), bf16),
            pltpu.VMEM((2 * wide, span), bf16),
            pltpu.VMEM((4 * wide, span), bf16),
            pltpu.VMEM(((REACH + 1) * wide, frames * LANES), jnp.float32),
            pltpu.VMEM((LANES, 2 * frames * 5 * LANES), bf16),
            pltpu.VMEM((parts, deep, LANES), jnp.float32),
            pltpu.VMEM((2 * parts * cells, deep), bf16),
            pltpu.VMEM((deep, frames * LANES), bf16),
            pltpu.VMEM((deep, frames * LANES), bf16),
            pltpu.SemaphoreType.DMA((n,)),
            pltpu.SemaphoreType.DMA((n,)),
            pltpu.SemaphoreType.DMA((3,)),
            pltpu.SemaphoreType.REGULAR((n,)),
        ],
        compiler_params=pltpu.CompilerParams(
            vmem_limit_bytes=(40 if n <= SMALL else 56) * 1024 * 1024, collective_id=0, has_side_effects=True
        ),
    )(
        stay(jnp.transpose(estimate, (0, 1, 3, 2, 4)).reshape(flat)),
        stay(jnp.transpose(measured, (0, 1, 3, 2, 4)).reshape(flat)),
        stay(sampled_lines),
    )
    return jnp.transpose(out.reshape(parts, coils, rows, frames, readout), (0, 1, 3, 2, 4))


def solution(mesh):
    placed = (
        P(None, None, "grp", "slab", None),
        P(None, None, "grp", "slab", None),
        P("grp", None),
    )
    return jax.shard_map(
        local,
        mesh=mesh,
        in_specs=placed,
        out_specs=P(None, None, "grp", "slab", None),
        check_vma=False,
    )
```

```python
import functools

import jax
import jax.numpy as jnp
from jax import lax
from jax.experimental import pallas as pl
from jax.experimental.pallas import tpu as pltpu
from jax.sharding import PartitionSpec as P

LANES = 128
REACH = 4
SPAN = range(-REACH, REACH + 1)
SMALL = 16


def couplings(frames):
    table = {}
    for s in range(frames):
        for s2 in range(frames):
            for d in range(1 - frames, frames):
                if 0 <= s + d < frames and 0 <= s2 + d < frames:
                    table[s, s2, d] = sum(
                        1
                        for t in range(frames)
                        if 0 <= t + d < frames and abs(s - t) <= 2 and abs(s2 - t) <= 2
                    )
    return {k: v for k, v in table.items() if v}


def halves(x):
    hi = x.astype(jnp.bfloat16)
    return hi, (x - hi.astype(jnp.float32)).astype(jnp.bfloat16)


def dot_nt(a, b):
    return lax.dot_general(a, b, (((1,), (1,)), ((), ())), preferred_element_type=jnp.float32)


def dot_nn(a, b):
    return lax.dot_general(a, b, (((1,), (0,)), ((), ())), preferred_element_type=jnp.float32)


def kernel(
    n, sizes, est_hbm, meas_hbm, picks_hbm, out_ref,
    est, meas, picks, all_ref, even, odd, base, sums, shift, flat, patch, u_hi, u_lo,
    send_sem, recv_sem, in_sem, ready,
):
    parts, frames, coils, rows, readout = sizes
    me = lax.axis_index("slab")
    flip = me >= n - 4
    mine = jnp.where(flip, n - 1 - me, me)
    total = n * rows
    ext = coils * 5
    wide = frames * ext
    bf16 = jnp.bfloat16

    loads = [
        pltpu.make_async_copy(est_hbm, est, in_sem.at[0]),
        pltpu.make_async_copy(meas_hbm, meas, in_sem.at[1]),
        pltpu.make_async_copy(picks_hbm, picks, in_sem.at[2]),
    ]
    for load in loads:
        load.start()

    def greet(j, carry):
        pl.semaphore_signal(pltpu.get_barrier_semaphore(), inc=1, device_id={"slab": j})
        return carry

    lax.fori_loop(me + 1, n, greet, 0)

    def place(line, s, part):
        return pl.ds((part * coils * rows + line) * frames + s, coils, stride=rows * frames)

    loads[0].wait()
    for j in range(rows):
        all_ref[me, j * coils : (j + 1) * coils, :] = jnp.concatenate(
            [est[place(j, s, part), :] for part in range(parts) for s in range(frames)], axis=1
        )
    pl.when(me > 0)(lambda: pl.semaphore_wait(pltpu.get_barrier_semaphore(), me))

    def copy(other, slot):
        return pltpu.make_async_remote_copy(
            src_ref=all_ref.at[slot],
            dst_ref=all_ref.at[slot],
            send_sem=send_sem.at[other],
            recv_sem=recv_sem.at[slot],
            device_id={"slab": other},
        )

    def down(j, carry):
        pl.semaphore_signal(ready.at[me], inc=1, device_id={"slab": j})
        copy(j, me).start()
        return carry

    lax.fori_loop(0, me, down, 0)

    def meet(j, carry):
        pl.semaphore_wait(ready.at[j], 1)
        copy(j, me).start()
        return carry

    first_group = me < 4

    def meet_group(t):
        stop = jnp.where(first_group, 4 * t + 4, me + 1)
        lax.fori_loop(jnp.where(first_group, jnp.maximum(me + 1, 4 * t), me + 1), stop, meet, 0)

    lax.fori_loop(me + 1, jnp.where(first_group, me + 1, n), meet, 0)
    meet_group(0)
    meet_group(1)

    def take(k):
        j = jnp.where(flip, n - 1 - k, k)
        pl.when(j != me)(lambda: copy(j, j).wait_recv())

    lane = lax.broadcasted_iota(jnp.int32, (1, LANES), 1)
    slot = lane // readout
    x = lane % readout
    second = slot >= parts
    turn = jnp.where(slot % parts == 0, 1.0, -1.0)
    nothing = jnp.zeros((coils, LANES), jnp.float32)

    def rolled(v, by):
        by = by % LANES
        return pltpu.roll(v, by, 1) if by else v

    def shifts(v):
        return [
            jnp.where((x + d >= 0) & (x + d < readout), rolled(v, -d), 0.0) if d else v
            for d in range(-2, 3)
        ]

    def line_block(line):
        if isinstance(line, int) and not 0 <= line < total:
            return nothing
        dev, j = line // rows, line % rows
        dev = jnp.where(flip, n - 1 - dev, dev)
        j = jnp.where(flip, rows - 1 - j, j)
        return all_ref[dev, pl.ds(pl.multiple_of(j * coils, coils), coils), :]

    order = [(s, e) for s in range(frames) for e in range(5)]

    def reach_of(line):
        inside = [(line - b >= 0) & (line - b < total) for b in range(-2, 3)]
        if isinstance(line, int):
            return float(sum(inside))
        return sum(jnp.where(v, 1.0, 0.0) for v in inside)

    def at_tile(i):
        start = (i // 2 + 2) * LANES
        return pl.ds(start if isinstance(i, int) else pl.multiple_of(start, LANES), LANES)

    pieces_of = len(order)
    row = lax.broadcasted_iota(jnp.int32, (LANES, LANES), 0)
    part_at = slot % parts
    for b, (s, e) in enumerate(order):
        for k, part in enumerate((part_at, 1 - part_at)):
            from_x = x + e - 2
            target = jnp.where(
                (from_x >= 0) & (from_x < readout), (part * frames + s) * readout + from_x, -1
            )
            one = 1.0 if k == 0 else turn
            shift[:, (k * pieces_of + b) * LANES : (k * pieces_of + b + 1) * LANES] = jnp.where(
                row == target, one, 0.0
            ).astype(bf16)

    def absorb(first, count, energy):
        lines = [line_block(first + k) for k in range(count + 1)]
        for k in range(1, count + 1):
            line = first + k
            if not isinstance(line, int) or line < total:
                energy = energy + reach_of(line) * (lines[k] * lines[k])
        raw = jnp.concatenate(lines, axis=0)
        high = raw.astype(bf16).astype(jnp.float32)
        split = jnp.concatenate([high, raw - high], axis=0).astype(bf16)
        g = dot_nn(split, shift[...])

        def piece(k, w, b):
            top = (w * (count + 1) + k) * coils
            return g[top : top + coils, b * LANES : (b + 1) * LANES]

        for step in range(count):
            i = first + step
            is_even = (step + PARITY) % 2 == 0
            tiles = even if is_even else odd
            at = at_tile(i)
            for w in range(2):
                cells = [
                    jnp.where(second, piece(step + 1, w, b), piece(step, w, b))
                    for b in range(pieces_of)
                ]
                tiles[w * wide : (w + 1) * wide, at] = jnp.concatenate(cells, axis=0).astype(bf16)
                if is_even and (not isinstance(i, int) or 0 <= i < total):
                    both = [
                        jnp.where(second, piece(step + 1, w, b), piece(step, w, b))
                        for b in range(pieces_of, 2 * pieces_of)
                    ]
                    stacked = []
                    for s in range(frames):
                        stacked += [cells[order.index((s, e))] for e in range(5)]
                        stacked += [both[order.index((s, e))] for e in range(5)]
                    base[w * 2 * wide : (w + 1) * 2 * wide, at] = jnp.concatenate(
                        stacked, axis=0
                    ).astype(bf16)
        return energy

    gap = jnp.zeros((LANES - 2 * ext, 1), bf16)

    def columns(at, w, count):
        pad = jnp.broadcast_to(gap, (LANES - 2 * ext, count * LANES))
        pieces = []
        for s in range(frames):
            top = w * 2 * wide + s * 2 * ext
            pieces += [base[top : top + 2 * ext, at], pad]
        return jnp.concatenate(pieces, axis=0)

    def lanes_from(tile, count):
        start = (tile + 2) * LANES
        return pl.ds(start if isinstance(tile, int) else pl.multiple_of(start, LANES), count * LANES)

    def stretch(i, w, count):
        tiles = even if i % 2 == 0 else odd
        return tiles[w * wide : (w + 1) * wide, lanes_from(i // 2, count)]

    def product(rows_hi, rows_lo, cols_hi, cols_lo):
        return dot_nt(
            jnp.concatenate([rows_hi, rows_lo, rows_hi], axis=1),
            jnp.concatenate([cols_hi, cols_hi, cols_lo], axis=1),
        )

    def gram(tile, count, fresh=False):
        at = lanes_from(tile, count)

        def moved(w):
            pieces = []
            for dy in range(REACH + 1):
                tiles = even if dy % 2 == 0 else odd
                pieces.append(tiles[w * wide : (w + 1) * wide, lanes_from(tile + dy // 2, count)])
            return jnp.concatenate(pieces, axis=0)

        g = product(moved(0), moved(1), columns(at, 0, count), columns(at, 1, count))
        sums[...] = g if fresh else sums[...] + g

    def edge(i):
        at = lanes_from(i // 2, 1)

        def picked(w):
            zero = jnp.zeros((wide, LANES), bf16)
            return jnp.concatenate(
                [
                    jnp.where(second, zero, stretch(i, w, 1)),
                    jnp.where(second, zero, stretch(i + 1, w, 1)),
                    jnp.where(second, stretch(i - 1, w, 1), zero),
                    jnp.where(second, stretch(i, w, 1), zero),
                ],
                axis=0,
            )

        return product(picked(0), picked(1), columns(at, 0, 1), columns(at, 1, 1))

    ahead = REACH + 1
    members = [(dy, None) for dy in (*range(ahead), *range(-1, -ahead, -1))]
    for i in (0, total - 2):
        members += [(0, i), (1, i), (-1, i + 1), (0, i + 1)]
    depth = len(members) * wide
    deep = -(-depth // LANES) * LANES
    cells_here = rows * readout

    def patches():
        line_at = mine * rows + slot

        def coefficient(dy, q=None):
            count = jnp.zeros((1, LANES), jnp.float32)
            for b in range(max(-2, -2 - dy), min(2, 2 - dy) + 1):
                if q is not None and 0 <= q - b < total:
                    continue
                count = count + jnp.where((line_at - b >= 0) & (line_at - b < total), 1.0, 0.0)
            return count if q is None else -count

        around = []
        for i in range(rows + 2 * REACH):
            line = mine * rows - REACH + i
            block = line_block(jnp.clip(line, 0, total - 1))
            block = jnp.where((line >= 0) & (line < total), block, 0.0)
            around.append([rolled(block, by * readout) for by in range(LANES // readout)])
        for dy in SPAN:
            for part in range(parts):
                cells = []
                for s in range(frames):
                    v = nothing
                    for j in range(rows):
                        seg = part * frames + s
                        v = jnp.where(slot == j, around[dy + REACH + j][(j - seg) % 4], v)
                    cells.append(shifts(v))
                v = jnp.concatenate([cells[s][e] for s, e in order], axis=0)
                for t, (dy2, q) in enumerate(members):
                    if dy2 == dy:
                        factor = float(couplings(frames)[0, 0, 0]) * coefficient(dy, q)
                        flat[part, t * wide : (t + 1) * wide, :] = factor * v
        for part in range(parts):
            for k in range(0, deep, LANES):
                hi, lo = halves(flat[part, k : k + LANES, :].T[:cells_here])
                at = pl.ds(k, LANES)
                patch[pl.ds(part * cells_here, cells_here), at] = hi
                patch[pl.ds((parts + part) * cells_here, cells_here), at] = lo

    table = couplings(frames)
    unit = float(table[0, 0, 0])

    def mixed(u):
        result = []
        for s2 in range(frames):
            pieces = []
            for s in range(frames):
                whole = None
                for d in range(1 - frames, frames):
                    if (s, s2, d) in table:
                        row = (s + d) * ext
                        term = u[row : row + ext, (s2 + d) * LANES : (s2 + d + 1) * LANES]
                        factor = table[s, s2, d] / unit
                        term = term if factor == 1 else factor * term
                        whole = term if whole is None else whole + term
                pieces.append(whole)
            result.append(jnp.concatenate(pieces, axis=0))
        return result

    def settle(t, cells):
        for s2 in range(frames):
            hi, lo = halves(cells[s2])
            at = pl.ds(s2 * LANES, LANES)
            u_hi[t * wide : (t + 1) * wide, at] = hi
            u_lo[t * wide : (t + 1) * wide, at] = lo

    def mirrored(cells):
        pieces = [[], []]
        for s in range(frames):
            spare = jnp.zeros((LANES - wide, LANES), jnp.float32)
            v = jnp.concatenate([cells[s], spare], axis=0).T
            re, im = v[:ext], v[ext : 2 * ext]
            pieces[0].append(jnp.where(lane < ext, re, -rolled(im, ext)))
            pieces[1].append(jnp.where(lane < ext, rolled(re, -ext), -im))
        return [jnp.concatenate(p, axis=0) for p in pieces]

    for i in (total, total + 1, total + 2):
        tiles = even if i % 2 == 0 else odd
        tiles[:, at_tile(i)] = jnp.zeros((2 * wide, LANES), bf16)
    for part in range(parts):
        flat[part, depth:deep, :] = jnp.zeros((deep - depth, LANES), jnp.float32)
    for ref in (u_hi, u_lo):
        ref[depth:deep, :] = jnp.zeros((deep - depth, frames * LANES), bf16)

    group = 4 * rows
    groups = n // 4
    half = group // 2

    def settle_edge(first, i):
        g = edge(i)
        for k in range(4):
            settle(first + k, mixed(g[k * wide : (k + 1) * wide]))

    energy = nothing
    PARITY = 1
    if n <= SMALL:
        for t in range(2, groups - 1):
            meet_group(t)
        seen, done = 0, 0
        for stop in (n // 2, n - 2, n):
            for k in range(seen, stop):
                take(k)
            first = seen * rows - 1
            PARITY = first % 2
            energy = absorb(first, (stop - seen) * rows + (stop == n), energy)
            reached = total if stop == n else (stop * rows - REACH) // 4 * 4
            gram(done // 2, (reached - done) // 2, fresh=done == 0)
            if seen == 0:
                settle_edge(len(SPAN), 0)
                meet_group(groups - 1)
            elif stop < n:
                patches()
            seen, done = stop, reached
    else:
        lax.fori_loop(2, groups, lambda t, c: (meet_group(t), c)[1], 0)

        def pairs(t):
            for k in range(4):
                take(4 * t + k)

        pairs(0)
        energy = absorb(-1, group, energy)
        gram(0, (group - REACH) // 2, fresh=True)
        settle_edge(len(SPAN), 0)

        def step(t, energy):
            pairs(t)
            energy = absorb(group * t - 1, group, energy)
            gram((group * t - REACH) // 2, group // 2)
            return energy

        energy = lax.fori_loop(1, groups - 1, step, energy)
        pairs(groups - 1)
        first = group * (groups - 1)
        energy = absorb(first - 1, group + 1, energy)
        gram((first - REACH) // 2, (group + REACH) // 2)
        patches()

    settle_edge(len(SPAN) + 4, total - 2)
    for t in range(ahead):
        cells = mixed(sums[t * wide : (t + 1) * wide, :])
        settle(t, cells)
        if t:
            settle(REACH + t, mirrored(cells))

    across = sum(jnp.where((x - d >= 0) & (x - d < readout), 1.0, 0.0) for d in range(-2, 3))
    frame = slot % frames
    for s in range(frames):
        reach = sum(1.0 for t in range(frames) if abs(s - t) <= 2)
        across = jnp.where(frame == s, across * reach, across)
    energy = jnp.sum(energy * across, axis=0, keepdims=True)
    scale = jnp.sum(energy, axis=1, keepdims=True) / (125 * coils) + 1e-06
    factor = 1.0 / (125.0 * scale)

    tall = parts * cells_here
    both = dot_nn(patch[...], u_hi[...])
    y = both[:tall] + both[tall:] + dot_nn(patch[0:tall, :], u_lo[...])

    for load in loads[1:]:
        load.wait()
    chosen = picks[...]
    spare = jnp.zeros((LANES - cells_here, LANES), jnp.float32)
    for s in range(frames):
        turned = []
        for part in range(parts):
            v = y[part * cells_here : (part + 1) * cells_here, s * LANES : (s + 1) * LANES]
            turned.append((jnp.concatenate([v, spare], axis=0) if cells_here < LANES else v).T)
        for part in range(parts):
            folded = nothing
            for e in range(5):
                plain = slice(e * coils, (e + 1) * coils)
                cross = slice(ext + e * coils, ext + (e + 1) * coils)
                if part == 0:
                    v = turned[0][plain] - turned[1][cross]
                else:
                    v = turned[0][cross] + turned[1][plain]
                d = e - 2
                v = jnp.where((x - d >= 0) & (x - d < readout), rolled(v, d), 0.0) if d else v
                folded = folded + v
            folded = folded * factor
            for j in range(rows):
                hit = jnp.where(chosen[s : s + 1, :] == me * rows + j, 1.0, 0.0)
                hit = jnp.max(hit, axis=1, keepdims=True)
                at = place(j, s, part)
                there = jnp.where(
                    flip, rolled(folded, (j + 1 - rows) * readout), rolled(folded, -j * readout)
                )
                out_ref[at, :] = jnp.where(hit > 0.5, meas[at, :], there[:, :readout])

    def finish(k, carry):
        copy(k + (k >= me).astype(jnp.int32), me).wait_send()
        return carry

    lax.fori_loop(0, n - 1, finish, 0)


def local(estimate, measured, sampled_lines):
    parts, coils, frames, rows, readout = estimate.shape
    n = lax.axis_size("slab")
    assert parts * frames * readout == LANES and frames == 2 and coils == 8
    assert rows * readout <= LANES and n % 4 == 0 and n >= 8 and 4 * rows >= 3 * REACH
    flat = (parts * coils * rows * frames, readout)
    total = n * rows
    wide = frames * 5 * coils
    span = (total // 2 + 4) * LANES
    deep = -(-(len(SPAN) + 8) * wide // LANES) * LANES
    cells = rows * readout
    bf16 = jnp.bfloat16
    stay = functools.partial(pltpu.with_memory_space_constraint, memory_space=pltpu.HBM)
    out = pl.pallas_call(
        functools.partial(kernel, n, (parts, frames, coils, rows, readout)),
        out_shape=jax.ShapeDtypeStruct(flat, jnp.float32),
        in_specs=[pl.BlockSpec(memory_space=pltpu.HBM)] * 3,
        out_specs=pl.BlockSpec(memory_space=pltpu.VMEM),
        scratch_shapes=[
            pltpu.VMEM(flat, jnp.float32),
            pltpu.VMEM(flat, jnp.float32),
            pltpu.VMEM(sampled_lines.shape, jnp.int32),
            pltpu.VMEM((n, rows * coils, LANES), jnp.float32),
            pltpu.VMEM((2 * wide, span), bf16),
            pltpu.VMEM((2 * wide, span), bf16),
            pltpu.VMEM((4 * wide, span), bf16),
            pltpu.VMEM(((REACH + 1) * wide, frames * LANES), jnp.float32),
            pltpu.VMEM((LANES, 2 * frames * 5 * LANES), bf16),
            pltpu.VMEM((parts, deep, LANES), jnp.float32),
            pltpu.VMEM((2 * parts * cells, deep), bf16),
            pltpu.VMEM((deep, frames * LANES), bf16),
            pltpu.VMEM((deep, frames * LANES), bf16),
            pltpu.SemaphoreType.DMA((n,)),
            pltpu.SemaphoreType.DMA((n,)),
            pltpu.SemaphoreType.DMA((3,)),
            pltpu.SemaphoreType.REGULAR((n,)),
        ],
        compiler_params=pltpu.CompilerParams(
            vmem_limit_bytes=(40 if n <= SMALL else 56) * 1024 * 1024, collective_id=0, has_side_effects=True
        ),
    )(
        stay(jnp.transpose(estimate, (0, 1, 3, 2, 4)).reshape(flat)),
        stay(jnp.transpose(measured, (0, 1, 3, 2, 4)).reshape(flat)),
        stay(sampled_lines),
    )
    return jnp.transpose(out.reshape(parts, coils, rows, frames, readout), (0, 1, 3, 2, 4))


def solution(mesh):
    placed = (
        P(None, None, "grp", "slab", None),
        P(None, None, "grp", "slab", None),
        P("grp", None),
    )
    return jax.shard_map(
        local,
        mesh=mesh,
        in_specs=placed,
        out_specs=P(None, None, "grp", "slab", None),
        check_vma=False,
    )
```

```python
import functools

import jax
import jax.numpy as jnp
from jax import lax
from jax.experimental import pallas as pl
from jax.experimental.pallas import tpu as pltpu
from jax.sharding import PartitionSpec as P

LANES = 128
REACH = 4
SPAN = range(-REACH, REACH + 1)
SMALL = 16


def couplings(frames):
    table = {}
    for s in range(frames):
        for s2 in range(frames):
            for d in range(1 - frames, frames):
                if 0 <= s + d < frames and 0 <= s2 + d < frames:
                    table[s, s2, d] = sum(
                        1
                        for t in range(frames)
                        if 0 <= t + d < frames and abs(s - t) <= 2 and abs(s2 - t) <= 2
                    )
    return {k: v for k, v in table.items() if v}


def halves(x):
    hi = x.astype(jnp.bfloat16)
    return hi, (x - hi.astype(jnp.float32)).astype(jnp.bfloat16)


def dot_nt(a, b):
    return lax.dot_general(a, b, (((1,), (1,)), ((), ())), preferred_element_type=jnp.float32)


def dot_nn(a, b):
    return lax.dot_general(a, b, (((1,), (0,)), ((), ())), preferred_element_type=jnp.float32)


def kernel(
    n, sizes, est_hbm, meas_hbm, picks_hbm, out_ref,
    est, meas, picks, all_ref, even, odd, base, sums, shift, flat, patch, u_hi, u_lo,
    send_sem, recv_sem, in_sem, ready,
):
    parts, frames, coils, rows, readout = sizes
    me = lax.axis_index("slab")
    flip = me >= n // 2
    mine = jnp.where(flip, n - 1 - me, me)
    total = n * rows
    ext = coils * 5
    wide = frames * ext
    bf16 = jnp.bfloat16

    loads = [
        pltpu.make_async_copy(est_hbm, est, in_sem.at[0]),
        pltpu.make_async_copy(meas_hbm, meas, in_sem.at[1]),
        pltpu.make_async_copy(picks_hbm, picks, in_sem.at[2]),
    ]
    for load in loads:
        load.start()

    def greet(j, carry):
        pl.semaphore_signal(pltpu.get_barrier_semaphore(), inc=1, device_id={"slab": j})
        return carry

    lax.fori_loop(me + 1, n, greet, 0)

    def place(line, s, part):
        return pl.ds((part * coils * rows + line) * frames + s, coils, stride=rows * frames)

    loads[0].wait()
    for j in range(rows):
        all_ref[me, j * coils : (j + 1) * coils, :] = jnp.concatenate(
            [est[place(j, s, part), :] for part in range(parts) for s in range(frames)], axis=1
        )
    pl.when(me > 0)(lambda: pl.semaphore_wait(pltpu.get_barrier_semaphore(), me))

    def copy(other, slot):
        return pltpu.make_async_remote_copy(
            src_ref=all_ref.at[slot],
            dst_ref=all_ref.at[slot],
            send_sem=send_sem.at[other],
            recv_sem=recv_sem.at[slot],
            device_id={"slab": other},
        )

    def down(j, carry):
        pl.semaphore_signal(ready.at[me], inc=1, device_id={"slab": j})
        copy(j, me).start()
        return carry

    lax.fori_loop(0, jnp.minimum(me, 4), down, 0)
    lax.fori_loop(4, me, lambda k, c: down(me + 3 - k, c), 0)

    def meet(j, carry):
        pl.semaphore_wait(ready.at[j], 1)
        copy(j, me).start()
        return carry

    first_group = me < 4

    def meet_group(t):
        stop = jnp.where(first_group, 4 * t + 4, me + 1)
        lax.fori_loop(jnp.where(first_group, jnp.maximum(me + 1, 4 * t), me + 1), stop, meet, 0)

    lax.fori_loop(me + 1, jnp.where(first_group, me + 1, n), meet, 0)
    meet_group(0)
    meet_group(1)

    def take(k):
        j = jnp.where(flip, n - 1 - k, k)
        pl.when(j != me)(lambda: copy(j, j).wait_recv())

    lane = lax.broadcasted_iota(jnp.int32, (1, LANES), 1)
    slot = lane // readout
    x = lane % readout
    second = slot >= parts
    turn = jnp.where(slot % parts == 0, 1.0, -1.0)
    nothing = jnp.zeros((coils, LANES), jnp.float32)

    def rolled(v, by):
        by = by % LANES
        return pltpu.roll(v, by, 1) if by else v

    def shifts(v):
        return [
            jnp.where((x + d >= 0) & (x + d < readout), rolled(v, -d), 0.0) if d else v
            for d in range(-2, 3)
        ]

    def line_block(line):
        if isinstance(line, int) and not 0 <= line < total:
            return nothing
        dev, j = line // rows, line % rows
        dev = jnp.where(flip, n - 1 - dev, dev)
        j = jnp.where(flip, rows - 1 - j, j)
        return all_ref[dev, pl.ds(pl.multiple_of(j * coils, coils), coils), :]

    order = [(s, e) for s in range(frames) for e in range(5)]

    def reach_of(line):
        inside = [(line - b >= 0) & (line - b < total) for b in range(-2, 3)]
        if isinstance(line, int):
            return float(sum(inside))
        return sum(jnp.where(v, 1.0, 0.0) for v in inside)

    def at_tile(i):
        start = (i // 2 + 2) * LANES
        return pl.ds(start if isinstance(i, int) else pl.multiple_of(start, LANES), LANES)

    pieces_of = len(order)
    row = lax.broadcasted_iota(jnp.int32, (LANES, LANES), 0)
    part_at = slot % parts
    for b, (s, e) in enumerate(order):
        for k, part in enumerate((part_at, 1 - part_at)):
            from_x = x + e - 2
            target = jnp.where(
                (from_x >= 0) & (from_x < readout), (part * frames + s) * readout + from_x, -1
            )
            one = 1.0 if k == 0 else turn
            shift[:, (k * pieces_of + b) * LANES : (k * pieces_of + b + 1) * LANES] = jnp.where(
                row == target, one, 0.0
            ).astype(bf16)

    def absorb(first, count, energy):
        lines = [line_block(first + k) for k in range(count + 1)]
        for k in range(1, count + 1):
            line = first + k
            if not isinstance(line, int) or line < total:
                energy = energy + reach_of(line) * (lines[k] * lines[k])
        raw = jnp.concatenate(lines, axis=0)
        high = raw.astype(bf16).astype(jnp.float32)
        split = jnp.concatenate([high, raw - high], axis=0).astype(bf16)
        g = dot_nn(split, shift[...])

        def piece(k, w, b):
            top = (w * (count + 1) + k) * coils
            return g[top : top + coils, b * LANES : (b + 1) * LANES]

        for step in range(count):
            i = first + step
            is_even = (step + PARITY) % 2 == 0
            tiles = even if is_even else odd
            at = at_tile(i)
            for w in range(2):
                cells = [
                    jnp.where(second, piece(step + 1, w, b), piece(step, w, b))
                    for b in range(pieces_of)
                ]
                tiles[w * wide : (w + 1) * wide, at] = jnp.concatenate(cells, axis=0).astype(bf16)
                if is_even and (not isinstance(i, int) or 0 <= i < total):
                    both = [
                        jnp.where(second, piece(step + 1, w, b), piece(step, w, b))
                        for b in range(pieces_of, 2 * pieces_of)
                    ]
                    stacked = []
                    for s in range(frames):
                        stacked += [cells[order.index((s, e))] for e in range(5)]
                        stacked += [both[order.index((s, e))] for e in range(5)]
                    base[w * 2 * wide : (w + 1) * 2 * wide, at] = jnp.concatenate(
                        stacked, axis=0
                    ).astype(bf16)
        return energy

    gap = jnp.zeros((LANES - 2 * ext, 1), bf16)

    def columns(at, w, count):
        pad = jnp.broadcast_to(gap, (LANES - 2 * ext, count * LANES))
        pieces = []
        for s in range(frames):
            top = w * 2 * wide + s * 2 * ext
            pieces += [base[top : top + 2 * ext, at], pad]
        return jnp.concatenate(pieces, axis=0)

    def lanes_from(tile, count):
        start = (tile + 2) * LANES
        return pl.ds(start if isinstance(tile, int) else pl.multiple_of(start, LANES), count * LANES)

    def stretch(i, w, count):
        tiles = even if i % 2 == 0 else odd
        return tiles[w * wide : (w + 1) * wide, lanes_from(i // 2, count)]

    def product(rows_hi, rows_lo, cols_hi, cols_lo):
        return dot_nt(
            jnp.concatenate([rows_hi, rows_lo, rows_hi], axis=1),
            jnp.concatenate([cols_hi, cols_hi, cols_lo], axis=1),
        )

    def gram(tile, count, fresh=False):
        at = lanes_from(tile, count)

        def moved(w):
            pieces = []
            for dy in range(REACH + 1):
                tiles = even if dy % 2 == 0 else odd
                pieces.append(tiles[w * wide : (w + 1) * wide, lanes_from(tile + dy // 2, count)])
            return jnp.concatenate(pieces, axis=0)

        g = product(moved(0), moved(1), columns(at, 0, count), columns(at, 1, count))
        sums[...] = g if fresh else sums[...] + g

    def edge(i):
        at = lanes_from(i // 2, 1)

        def picked(w):
            zero = jnp.zeros((wide, LANES), bf16)
            return jnp.concatenate(
                [
                    jnp.where(second, zero, stretch(i, w, 1)),
                    jnp.where(second, zero, stretch(i + 1, w, 1)),
                    jnp.where(second, stretch(i - 1, w, 1), zero),
                    jnp.where(second, stretch(i, w, 1), zero),
                ],
                axis=0,
            )

        return product(picked(0), picked(1), columns(at, 0, 1), columns(at, 1, 1))

    ahead = REACH + 1
    members = [(dy, None) for dy in (*range(ahead), *range(-1, -ahead, -1))]
    for i in (0, total - 2):
        members += [(0, i), (1, i), (-1, i + 1), (0, i + 1)]
    depth = len(members) * wide
    deep = -(-depth // LANES) * LANES
    cells_here = rows * readout

    def patches():
        line_at = mine * rows + slot

        def coefficient(dy, q=None):
            count = jnp.zeros((1, LANES), jnp.float32)
            for b in range(max(-2, -2 - dy), min(2, 2 - dy) + 1):
                if q is not None and 0 <= q - b < total:
                    continue
                count = count + jnp.where((line_at - b >= 0) & (line_at - b < total), 1.0, 0.0)
            return count if q is None else -count

        around = []
        for i in range(rows + 2 * REACH):
            line = mine * rows - REACH + i
            block = line_block(jnp.clip(line, 0, total - 1))
            block = jnp.where((line >= 0) & (line < total), block, 0.0)
            around.append([rolled(block, by * readout) for by in range(LANES // readout)])
        for dy in SPAN:
            for part in range(parts):
                cells = []
                for s in range(frames):
                    v = nothing
                    for j in range(rows):
                        seg = part * frames + s
                        v = jnp.where(slot == j, around[dy + REACH + j][(j - seg) % 4], v)
                    cells.append(shifts(v))
                v = jnp.concatenate([cells[s][e] for s, e in order], axis=0)
                for t, (dy2, q) in enumerate(members):
                    if dy2 == dy:
                        factor = float(couplings(frames)[0, 0, 0]) * coefficient(dy, q)
                        flat[part, t * wide : (t + 1) * wide, :] = factor * v
        for part in range(parts):
            for k in range(0, deep, LANES):
                hi, lo = halves(flat[part, k : k + LANES, :].T[:cells_here])
                at = pl.ds(k, LANES)
                patch[pl.ds(part * cells_here, cells_here), at] = hi
                patch[pl.ds((parts + part) * cells_here, cells_here), at] = lo

    table = couplings(frames)
    unit = float(table[0, 0, 0])

    def mixed(u):
        result = []
        for s2 in range(frames):
            pieces = []
            for s in range(frames):
                whole = None
                for d in range(1 - frames, frames):
                    if (s, s2, d) in table:
                        row = (s + d) * ext
                        term = u[row : row + ext, (s2 + d) * LANES : (s2 + d + 1) * LANES]
                        factor = table[s, s2, d] / unit
                        term = term if factor == 1 else factor * term
                        whole = term if whole is None else whole + term
                pieces.append(whole)
            result.append(jnp.concatenate(pieces, axis=0))
        return result

    def settle(t, cells):
        for s2 in range(frames):
            hi, lo = halves(cells[s2])
            at = pl.ds(s2 * LANES, LANES)
            u_hi[t * wide : (t + 1) * wide, at] = hi
            u_lo[t * wide : (t + 1) * wide, at] = lo

    def mirrored(cells):
        pieces = [[], []]
        for s in range(frames):
            spare = jnp.zeros((LANES - wide, LANES), jnp.float32)
            v = jnp.concatenate([cells[s], spare], axis=0).T
            re, im = v[:ext], v[ext : 2 * ext]
            pieces[0].append(jnp.where(lane < ext, re, -rolled(im, ext)))
            pieces[1].append(jnp.where(lane < ext, rolled(re, -ext), -im))
        return [jnp.concatenate(p, axis=0) for p in pieces]

    tall = parts * cells_here

    def filtered(first, count):
        at = pl.ds(first * wide, count * wide)
        both = dot_nn(patch[:, at], u_hi[at, :])
        return both[:tall] + both[tall:] + dot_nn(patch[0:tall, at], u_lo[at, :])

    for i in (total, total + 1, total + 2):
        tiles = even if i % 2 == 0 else odd
        tiles[:, at_tile(i)] = jnp.zeros((2 * wide, LANES), bf16)
    for part in range(parts):
        flat[part, depth:deep, :] = jnp.zeros((deep - depth, LANES), jnp.float32)
    for ref in (u_hi, u_lo):
        ref[depth:deep, :] = jnp.zeros((deep - depth, frames * LANES), bf16)

    group = 4 * rows
    groups = n // 4
    half = group // 2

    def settle_edge(first, i):
        g = edge(i)
        for k in range(4):
            settle(first + k, mixed(g[k * wide : (k + 1) * wide]))

    energy = nothing
    early = []
    PARITY = 1
    if n <= SMALL:
        for t in range(2, groups - 1):
            meet_group(t)
        seen, done = 0, 0
        for stop in (n // 2, n - 2, n):
            for k in range(seen, stop):
                take(k)
            first = seen * rows - 1
            PARITY = first % 2
            energy = absorb(first, (stop - seen) * rows + (stop == n), energy)
            if seen == 0:
                meet_group(groups - 1)
            reached = total if stop == n else (stop * rows - REACH) // 4 * 4
            gram(done // 2, (reached - done) // 2, fresh=done == 0)
            if seen == 0:
                settle_edge(len(SPAN), 0)
            elif stop < n:
                patches()
                early.append(filtered(len(SPAN), 4))
            seen, done = stop, reached
    else:
        lax.fori_loop(2, groups, lambda t, c: (meet_group(t), c)[1], 0)

        def pairs(t):
            for k in range(4):
                take(4 * t + k)

        pairs(0)
        energy = absorb(-1, group, energy)
        gram(0, (group - REACH) // 2, fresh=True)
        settle_edge(len(SPAN), 0)

        def step(t, energy):
            pairs(t)
            energy = absorb(group * t - 1, group, energy)
            gram((group * t - REACH) // 2, group // 2)
            return energy

        energy = lax.fori_loop(1, groups - 1, step, energy)
        pairs(groups - 1)
        first = group * (groups - 1)
        energy = absorb(first - 1, group + 1, energy)
        gram((first - REACH) // 2, (group + REACH) // 2)
        patches()

    settle_edge(len(SPAN) + 4, total - 2)
    for t in range(ahead):
        cells = mixed(sums[t * wide : (t + 1) * wide, :])
        settle(t, cells)
        if t:
            settle(REACH + t, mirrored(cells))

    across = sum(jnp.where((x - d >= 0) & (x - d < readout), 1.0, 0.0) for d in range(-2, 3))
    frame = slot % frames
    for s in range(frames):
        reach = sum(1.0 for t in range(frames) if abs(s - t) <= 2)
        across = jnp.where(frame == s, across * reach, across)
    energy = jnp.sum(energy * across, axis=0, keepdims=True)
    scale = jnp.sum(energy, axis=1, keepdims=True) / (125 * coils) + 1e-06
    factor = 1.0 / (125.0 * scale)

    y = filtered(0, len(SPAN)) + filtered(len(SPAN) + 4, 4)
    for part in early or [filtered(len(SPAN), 4)]:
        y = y + part

    for load in loads[1:]:
        load.wait()
    chosen = picks[...]
    spare = jnp.zeros((LANES - cells_here, LANES), jnp.float32)
    for s in range(frames):
        turned = []
        for part in range(parts):
            v = y[part * cells_here : (part + 1) * cells_here, s * LANES : (s + 1) * LANES]
            turned.append((jnp.concatenate([v, spare], axis=0) if cells_here < LANES else v).T)
        for part in range(parts):
            folded = nothing
            for e in range(5):
                plain = slice(e * coils, (e + 1) * coils)
                cross = slice(ext + e * coils, ext + (e + 1) * coils)
                if part == 0:
                    v = turned[0][plain] - turned[1][cross]
                else:
                    v = turned[0][cross] + turned[1][plain]
                d = e - 2
                v = jnp.where((x - d >= 0) & (x - d < readout), rolled(v, d), 0.0) if d else v
                folded = folded + v
            folded = folded * factor
            for j in range(rows):
                hit = jnp.where(chosen[s : s + 1, :] == me * rows + j, 1.0, 0.0)
                hit = jnp.max(hit, axis=1, keepdims=True)
                at = place(j, s, part)
                there = jnp.where(
                    flip, rolled(folded, (j + 1 - rows) * readout), rolled(folded, -j * readout)
                )
                out_ref[at, :] = jnp.where(hit > 0.5, meas[at, :], there[:, :readout])

    def finish(k, carry):
        copy(k + (k >= me).astype(jnp.int32), me).wait_send()
        return carry

    lax.fori_loop(0, n - 1, finish, 0)


def local(estimate, measured, sampled_lines):
    parts, coils, frames, rows, readout = estimate.shape
    n = lax.axis_size("slab")
    assert parts * frames * readout == LANES and frames == 2 and coils == 8
    assert rows * readout <= LANES and n % 4 == 0 and n >= 8 and 4 * rows >= 3 * REACH
    flat = (parts * coils * rows * frames, readout)
    total = n * rows
    wide = frames * 5 * coils
    span = (total // 2 + 4) * LANES
    deep = -(-(len(SPAN) + 8) * wide // LANES) * LANES
    cells = rows * readout
    bf16 = jnp.bfloat16
    stay = functools.partial(pltpu.with_memory_space_constraint, memory_space=pltpu.HBM)
    out = pl.pallas_call(
        functools.partial(kernel, n, (parts, frames, coils, rows, readout)),
        out_shape=jax.ShapeDtypeStruct(flat, jnp.float32),
        in_specs=[pl.BlockSpec(memory_space=pltpu.HBM)] * 3,
        out_specs=pl.BlockSpec(memory_space=pltpu.VMEM),
        scratch_shapes=[
            pltpu.VMEM(flat, jnp.float32),
            pltpu.VMEM(flat, jnp.float32),
            pltpu.VMEM(sampled_lines.shape, jnp.int32),
            pltpu.VMEM((n, rows * coils, LANES), jnp.float32),
            pltpu.VMEM((2 * wide, span), bf16),
            pltpu.VMEM((2 * wide, span), bf16),
            pltpu.VMEM((4 * wide, span), bf16),
            pltpu.VMEM(((REACH + 1) * wide, frames * LANES), jnp.float32),
            pltpu.VMEM((LANES, 2 * frames * 5 * LANES), bf16),
            pltpu.VMEM((parts, deep, LANES), jnp.float32),
            pltpu.VMEM((2 * parts * cells, deep), bf16),
            pltpu.VMEM((deep, frames * LANES), bf16),
            pltpu.VMEM((deep, frames * LANES), bf16),
            pltpu.SemaphoreType.DMA((n,)),
            pltpu.SemaphoreType.DMA((n,)),
            pltpu.SemaphoreType.DMA((3,)),
            pltpu.SemaphoreType.REGULAR((n,)),
        ],
        compiler_params=pltpu.CompilerParams(
            vmem_limit_bytes=(40 if n <= SMALL else 56) * 1024 * 1024, collective_id=0, has_side_effects=True
        ),
    )(
        stay(jnp.transpose(estimate, (0, 1, 3, 2, 4)).reshape(flat)),
        stay(jnp.transpose(measured, (0, 1, 3, 2, 4)).reshape(flat)),
        stay(sampled_lines),
    )
    return jnp.transpose(out.reshape(parts, coils, rows, frames, readout), (0, 1, 3, 2, 4))


def solution(mesh):
    placed = (
        P(None, None, "grp", "slab", None),
        P(None, None, "grp", "slab", None),
        P("grp", None),
    )
    return jax.shard_map(
        local,
        mesh=mesh,
        in_specs=placed,
        out_specs=P(None, None, "grp", "slab", None),
        check_vma=False,
    )
```

```python
import functools

import jax
import jax.numpy as jnp
from jax import lax
from jax.experimental import pallas as pl
from jax.experimental.pallas import tpu as pltpu
from jax.sharding import PartitionSpec as P

LANES = 128
REACH = 4
SPAN = range(-REACH, REACH + 1)
SMALL = 16


def couplings(frames):
    table = {}
    for s in range(frames):
        for s2 in range(frames):
            for d in range(1 - frames, frames):
                if 0 <= s + d < frames and 0 <= s2 + d < frames:
                    table[s, s2, d] = sum(
                        1
                        for t in range(frames)
                        if 0 <= t + d < frames and abs(s - t) <= 2 and abs(s2 - t) <= 2
                    )
    return {k: v for k, v in table.items() if v}


def halves(x):
    hi = x.astype(jnp.bfloat16)
    return hi, (x - hi.astype(jnp.float32)).astype(jnp.bfloat16)


def dot_nt(a, b):
    return lax.dot_general(a, b, (((1,), (1,)), ((), ())), preferred_element_type=jnp.float32)


def dot_nn(a, b):
    return lax.dot_general(a, b, (((1,), (0,)), ((), ())), preferred_element_type=jnp.float32)


def kernel(
    n, sizes, est_hbm, meas_hbm, picks_hbm, out_ref,
    est, meas, picks, all_ref, even, odd, base, sums, shift, flat, patch, u_hi, u_lo,
    send_sem, recv_sem, in_sem, ready,
):
    parts, frames, coils, rows, readout = sizes
    me = lax.axis_index("slab")
    flip = me >= n // 2
    mine = jnp.where(flip, n - 1 - me, me)
    total = n * rows
    ext = coils * 5
    wide = frames * ext
    bf16 = jnp.bfloat16

    loads = [
        pltpu.make_async_copy(est_hbm, est, in_sem.at[0]),
        pltpu.make_async_copy(meas_hbm, meas, in_sem.at[1]),
        pltpu.make_async_copy(picks_hbm, picks, in_sem.at[2]),
    ]
    for load in loads:
        load.start()

    def greet(j, carry):
        pl.semaphore_signal(pltpu.get_barrier_semaphore(), inc=1, device_id={"slab": j})
        return carry

    lax.fori_loop(me + 1, n, greet, 0)

    def place(line, s, part):
        return pl.ds((part * coils * rows + line) * frames + s, coils, stride=rows * frames)

    loads[0].wait()
    for j in range(rows):
        all_ref[me, j * coils : (j + 1) * coils, :] = jnp.concatenate(
            [est[place(j, s, part), :] for part in range(parts) for s in range(frames)], axis=1
        )
    pl.when(me > 0)(lambda: pl.semaphore_wait(pltpu.get_barrier_semaphore(), me))

    def copy(other, slot):
        return pltpu.make_async_remote_copy(
            src_ref=all_ref.at[slot],
            dst_ref=all_ref.at[slot],
            send_sem=send_sem,
            recv_sem=recv_sem.at[slot],
            device_id={"slab": other},
        )

    def down(j, carry):
        pl.semaphore_signal(ready.at[me], inc=1, device_id={"slab": j})
        copy(j, me).start()
        return carry

    def down_group(t, carry):
        g = me // 4 - t
        return lax.fori_loop(4 * g, jnp.minimum(4 * g + 4, me), down, carry)

    lax.fori_loop(0, jnp.minimum(me, 4), down, 0)
    lax.fori_loop(0, me // 4, down_group, 0)

    def meet(j, carry):
        pl.semaphore_wait(ready.at[j], 1)
        copy(j, me).start()
        return carry

    first_group = me < 4

    def meet_group(t):
        stop = jnp.where(first_group, 4 * t + 4, me + 1)
        lax.fori_loop(jnp.where(first_group, jnp.maximum(me + 1, 4 * t), me + 1), stop, meet, 0)

    lax.fori_loop(me + 1, jnp.where(first_group, me + 1, n), meet, 0)
    meet_group(0)
    meet_group(1)

    def take(k):
        j = jnp.where(flip, n - 1 - k, k)
        pl.when(j != me)(lambda: copy(j, j).wait_recv())

    lane = lax.broadcasted_iota(jnp.int32, (1, LANES), 1)
    slot = lane // readout
    x = lane % readout
    second = slot >= parts
    turn = jnp.where(slot % parts == 0, 1.0, -1.0)
    nothing = jnp.zeros((coils, LANES), jnp.float32)

    def rolled(v, by):
        by = by % LANES
        return pltpu.roll(v, by, 1) if by else v

    def shifts(v):
        return [
            jnp.where((x + d >= 0) & (x + d < readout), rolled(v, -d), 0.0) if d else v
            for d in range(-2, 3)
        ]

    def line_block(line):
        if isinstance(line, int) and not 0 <= line < total:
            return nothing
        dev, j = line // rows, line % rows
        dev = jnp.where(flip, n - 1 - dev, dev)
        j = jnp.where(flip, rows - 1 - j, j)
        return all_ref[dev, pl.ds(pl.multiple_of(j * coils, coils), coils), :]

    order = [(s, e) for s in range(frames) for e in range(5)]

    def reach_of(line):
        inside = [(line - b >= 0) & (line - b < total) for b in range(-2, 3)]
        if isinstance(line, int):
            return float(sum(inside))
        return sum(jnp.where(v, 1.0, 0.0) for v in inside)

    def at_tile(i):
        start = (i // 2 + 2) * LANES
        return pl.ds(start if isinstance(i, int) else pl.multiple_of(start, LANES), LANES)

    pieces_of = len(order)
    row = lax.broadcasted_iota(jnp.int32, (LANES, LANES), 0)
    part_at = slot % parts
    for b, (s, e) in enumerate(order):
        for k, part in enumerate((part_at, 1 - part_at)):
            from_x = x + e - 2
            target = jnp.where(
                (from_x >= 0) & (from_x < readout), (part * frames + s) * readout + from_x, -1
            )
            one = 1.0 if k == 0 else turn
            shift[:, (k * pieces_of + b) * LANES : (k * pieces_of + b + 1) * LANES] = jnp.where(
                row == target, one, 0.0
            ).astype(bf16)

    def absorb(first, count, energy):
        lines = [line_block(first + k) for k in range(count + 1)]
        for k in range(1, count + 1):
            line = first + k
            if not isinstance(line, int) or line < total:
                energy = energy + reach_of(line) * (lines[k] * lines[k])
        raw = jnp.concatenate(lines, axis=0)
        high = raw.astype(bf16).astype(jnp.float32)
        split = jnp.concatenate([high, raw - high], axis=0).astype(bf16)
        g = dot_nn(split, shift[...])

        def piece(k, w, b):
            top = (w * (count + 1) + k) * coils
            return g[top : top + coils, b * LANES : (b + 1) * LANES]

        for step in range(count):
            i = first + step
            is_even = (step + PARITY) % 2 == 0
            tiles = even if is_even else odd
            at = at_tile(i)
            for w in range(2):
                cells = [
                    jnp.where(second, piece(step + 1, w, b), piece(step, w, b))
                    for b in range(pieces_of)
                ]
                tiles[w * wide : (w + 1) * wide, at] = jnp.concatenate(cells, axis=0).astype(bf16)
                if is_even and (not isinstance(i, int) or 0 <= i < total):
                    both = [
                        jnp.where(second, piece(step + 1, w, b), piece(step, w, b))
                        for b in range(pieces_of, 2 * pieces_of)
                    ]
                    stacked = []
                    for s in range(frames):
                        stacked += [cells[order.index((s, e))] for e in range(5)]
                        stacked += [both[order.index((s, e))] for e in range(5)]
                    base[w * 2 * wide : (w + 1) * 2 * wide, at] = jnp.concatenate(
                        stacked, axis=0
                    ).astype(bf16)
        return energy

    gap = jnp.zeros((LANES - 2 * ext, 1), bf16)

    def columns(at, w, count):
        pad = jnp.broadcast_to(gap, (LANES - 2 * ext, count * LANES))
        pieces = []
        for s in range(frames):
            top = w * 2 * wide + s * 2 * ext
            pieces += [base[top : top + 2 * ext, at], pad]
        return jnp.concatenate(pieces, axis=0)

    def lanes_from(tile, count):
        start = (tile + 2) * LANES
        return pl.ds(start if isinstance(tile, int) else pl.multiple_of(start, LANES), count * LANES)

    def stretch(i, w, count):
        tiles = even if i % 2 == 0 else odd
        return tiles[w * wide : (w + 1) * wide, lanes_from(i // 2, count)]

    def product(rows_hi, rows_lo, cols_hi, cols_lo):
        return dot_nt(
            jnp.concatenate([rows_hi, rows_lo, rows_hi], axis=1),
            jnp.concatenate([cols_hi, cols_hi, cols_lo], axis=1),
        )

    def gram(tile, count, fresh=False):
        at = lanes_from(tile, count)

        def moved(w):
            pieces = []
            for dy in range(REACH + 1):
                tiles = even if dy % 2 == 0 else odd
                pieces.append(tiles[w * wide : (w + 1) * wide, lanes_from(tile + dy // 2, count)])
            return jnp.concatenate(pieces, axis=0)

        g = product(moved(0), moved(1), columns(at, 0, count), columns(at, 1, count))
        sums[...] = g if fresh else sums[...] + g

    def edge(i):
        at = lanes_from(i // 2, 1)

        def picked(w):
            zero = jnp.zeros((wide, LANES), bf16)
            return jnp.concatenate(
                [
                    jnp.where(second, zero, stretch(i, w, 1)),
                    jnp.where(second, zero, stretch(i + 1, w, 1)),
                    jnp.where(second, stretch(i - 1, w, 1), zero),
                    jnp.where(second, stretch(i, w, 1), zero),
                ],
                axis=0,
            )

        return product(picked(0), picked(1), columns(at, 0, 1), columns(at, 1, 1))

    ahead = REACH + 1
    members = [(dy, None) for dy in (*range(ahead), *range(-1, -ahead, -1))]
    for i in (0, total - 2):
        members += [(0, i), (1, i), (-1, i + 1), (0, i + 1)]
    depth = len(members) * wide
    deep = -(-depth // LANES) * LANES
    cells_here = rows * readout

    def patches():
        line_at = mine * rows + slot

        def coefficient(dy, q=None):
            count = jnp.zeros((1, LANES), jnp.float32)
            for b in range(max(-2, -2 - dy), min(2, 2 - dy) + 1):
                if q is not None and 0 <= q - b < total:
                    continue
                count = count + jnp.where((line_at - b >= 0) & (line_at - b < total), 1.0, 0.0)
            return count if q is None else -count

        around = []
        for i in range(rows + 2 * REACH):
            line = mine * rows - REACH + i
            block = line_block(jnp.clip(line, 0, total - 1))
            block = jnp.where((line >= 0) & (line < total), block, 0.0)
            around.append([rolled(block, by * readout) for by in range(LANES // readout)])
        for dy in SPAN:
            for part in range(parts):
                cells = []
                for s in range(frames):
                    v = nothing
                    for j in range(rows):
                        seg = part * frames + s
                        v = jnp.where(slot == j, around[dy + REACH + j][(j - seg) % 4], v)
                    cells.append(shifts(v))
                v = jnp.concatenate([cells[s][e] for s, e in order], axis=0)
                for t, (dy2, q) in enumerate(members):
                    if dy2 == dy:
                        factor = float(couplings(frames)[0, 0, 0]) * coefficient(dy, q)
                        flat[part, t * wide : (t + 1) * wide, :] = factor * v
        for part in range(parts):
            for k in range(0, deep, LANES):
                hi, lo = halves(flat[part, k : k + LANES, :].T[:cells_here])
                at = pl.ds(k, LANES)
                patch[pl.ds(part * cells_here, cells_here), at] = hi
                patch[pl.ds((parts + part) * cells_here, cells_here), at] = lo

    table = couplings(frames)
    unit = float(table[0, 0, 0])

    def mixed(u):
        result = []
        for s2 in range(frames):
            pieces = []
            for s in range(frames):
                whole = None
                for d in range(1 - frames, frames):
                    if (s, s2, d) in table:
                        row = (s + d) * ext
                        term = u[row : row + ext, (s2 + d) * LANES : (s2 + d + 1) * LANES]
                        factor = table[s, s2, d] / unit
                        term = term if factor == 1 else factor * term
                        whole = term if whole is None else whole + term
                pieces.append(whole)
            result.append(jnp.concatenate(pieces, axis=0))
        return result

    def settle(t, cells):
        for s2 in range(frames):
            hi, lo = halves(cells[s2])
            at = pl.ds(s2 * LANES, LANES)
            u_hi[t * wide : (t + 1) * wide, at] = hi
            u_lo[t * wide : (t + 1) * wide, at] = lo

    def mirrored(cells):
        pieces = [[], []]
        for s in range(frames):
            spare = jnp.zeros((LANES - wide, LANES), jnp.float32)
            v = jnp.concatenate([cells[s], spare], axis=0).T
            re, im = v[:ext], v[ext : 2 * ext]
            pieces[0].append(jnp.where(lane < ext, re, -rolled(im, ext)))
            pieces[1].append(jnp.where(lane < ext, rolled(re, -ext), -im))
        return [jnp.concatenate(p, axis=0) for p in pieces]

    tall = parts * cells_here

    def filtered(first, count):
        at = pl.ds(first * wide, count * wide)
        both = dot_nn(patch[:, at], u_hi[at, :])
        return both[:tall] + both[tall:] + dot_nn(patch[0:tall, at], u_lo[at, :])

    for i in (total, total + 1, total + 2):
        tiles = even if i % 2 == 0 else odd
        tiles[:, at_tile(i)] = jnp.zeros((2 * wide, LANES), bf16)
    for part in range(parts):
        flat[part, depth:deep, :] = jnp.zeros((deep - depth, LANES), jnp.float32)
    for ref in (u_hi, u_lo):
        ref[depth:deep, :] = jnp.zeros((deep - depth, frames * LANES), bf16)

    group = 4 * rows
    groups = n // 4
    half = group // 2

    def settle_edge(first, i):
        g = edge(i)
        for k in range(4):
            settle(first + k, mixed(g[k * wide : (k + 1) * wide]))

    for load in loads[1:]:
        load.wait()
    energy = nothing
    early = []
    PARITY = 1
    if n <= SMALL:
        for t in range(2, groups - 1):
            meet_group(t)
        seen, done = 0, 0
        for stop in (n // 4, n // 2, n - 2, n):
            for k in range(seen, stop):
                take(k)
            first = seen * rows - 1
            PARITY = first % 2
            energy = absorb(first, (stop - seen) * rows + (stop == n), energy)
            if stop == n // 2:
                meet_group(groups - 1)
            if stop in (n // 2, n - 2, n):
                reached = total if stop == n else (stop * rows - REACH) // 4 * 4
                gram(done // 2, (reached - done) // 2, fresh=done == 0)
                done = reached
            if seen == 0:
                settle_edge(len(SPAN), 0)
            if stop == n - 2:
                patches()
                early.append(filtered(len(SPAN), 4))
            seen = stop
    else:
        lax.fori_loop(2, groups, lambda t, c: (meet_group(t), c)[1], 0)

        def pairs(t):
            for k in range(4):
                take(4 * t + k)

        pairs(0)
        energy = absorb(-1, group, energy)
        gram(0, (group - REACH) // 2, fresh=True)
        settle_edge(len(SPAN), 0)

        def step(t, energy):
            pairs(t)
            energy = absorb(group * t - 1, group, energy)
            gram((group * t - REACH) // 2, group // 2)
            return energy

        energy = lax.fori_loop(1, groups - 1, step, energy)
        pairs(groups - 1)
        first = group * (groups - 1)
        energy = absorb(first - 1, group + 1, energy)
        gram((first - REACH) // 2, (group + REACH) // 2)
        patches()

    settle_edge(len(SPAN) + 4, total - 2)
    for t in range(ahead):
        cells = mixed(sums[t * wide : (t + 1) * wide, :])
        settle(t, cells)
        if t:
            settle(REACH + t, mirrored(cells))

    across = sum(jnp.where((x - d >= 0) & (x - d < readout), 1.0, 0.0) for d in range(-2, 3))
    frame = slot % frames
    for s in range(frames):
        reach = sum(1.0 for t in range(frames) if abs(s - t) <= 2)
        across = jnp.where(frame == s, across * reach, across)
    energy = jnp.sum(energy * across, axis=0, keepdims=True)
    scale = jnp.sum(energy, axis=1, keepdims=True) / (125 * coils) + 1e-06
    factor = 1.0 / (125.0 * scale)

    y = filtered(0, len(SPAN)) + filtered(len(SPAN) + 4, 4)
    for part in early or [filtered(len(SPAN), 4)]:
        y = y + part

    chosen = picks[...]
    spare = jnp.zeros((LANES - cells_here, LANES), jnp.float32)
    for s in range(frames):
        turned = []
        for part in range(parts):
            v = y[part * cells_here : (part + 1) * cells_here, s * LANES : (s + 1) * LANES]
            turned.append((jnp.concatenate([v, spare], axis=0) if cells_here < LANES else v).T)
        for part in range(parts):
            folded = nothing
            for e in range(5):
                plain = slice(e * coils, (e + 1) * coils)
                cross = slice(ext + e * coils, ext + (e + 1) * coils)
                if part == 0:
                    v = turned[0][plain] - turned[1][cross]
                else:
                    v = turned[0][cross] + turned[1][plain]
                d = e - 2
                v = jnp.where((x - d >= 0) & (x - d < readout), rolled(v, d), 0.0) if d else v
                folded = folded + v
            folded = folded * factor
            for j in range(rows):
                hit = jnp.where(chosen[s : s + 1, :] == me * rows + j, 1.0, 0.0)
                hit = jnp.max(hit, axis=1, keepdims=True)
                at = place(j, s, part)
                there = jnp.where(
                    flip, rolled(folded, (j + 1 - rows) * readout), rolled(folded, -j * readout)
                )
                out_ref[at, :] = jnp.where(hit > 0.5, meas[at, :], there[:, :readout])

    others = all_ref.at[pl.ds(0, n - 1)]
    pltpu.make_async_remote_copy(
        src_ref=others,
        dst_ref=others,
        send_sem=send_sem,
        recv_sem=recv_sem.at[me],
        device_id={"slab": lax.rem(me + 1, n)},
    ).wait_send()


def local(estimate, measured, sampled_lines):
    parts, coils, frames, rows, readout = estimate.shape
    n = lax.axis_size("slab")
    assert parts * frames * readout == LANES and frames == 2 and coils == 8
    assert rows * readout <= LANES and n % 4 == 0 and n >= 8 and 4 * rows >= 3 * REACH
    flat = (parts * coils * rows * frames, readout)
    total = n * rows
    wide = frames * 5 * coils
    span = (total // 2 + 4) * LANES
    deep = -(-(len(SPAN) + 8) * wide // LANES) * LANES
    cells = rows * readout
    bf16 = jnp.bfloat16
    stay = functools.partial(pltpu.with_memory_space_constraint, memory_space=pltpu.HBM)
    out = pl.pallas_call(
        functools.partial(kernel, n, (parts, frames, coils, rows, readout)),
        out_shape=jax.ShapeDtypeStruct(flat, jnp.float32),
        in_specs=[pl.BlockSpec(memory_space=pltpu.HBM)] * 3,
        out_specs=pl.BlockSpec(memory_space=pltpu.VMEM),
        scratch_shapes=[
            pltpu.VMEM(flat, jnp.float32),
            pltpu.VMEM(flat, jnp.float32),
            pltpu.VMEM(sampled_lines.shape, jnp.int32),
            pltpu.VMEM((n, rows * coils, LANES), jnp.float32),
            pltpu.VMEM((2 * wide, span), bf16),
            pltpu.VMEM((2 * wide, span), bf16),
            pltpu.VMEM((4 * wide, span), bf16),
            pltpu.VMEM(((REACH + 1) * wide, frames * LANES), jnp.float32),
            pltpu.VMEM((LANES, 2 * frames * 5 * LANES), bf16),
            pltpu.VMEM((parts, deep, LANES), jnp.float32),
            pltpu.VMEM((2 * parts * cells, deep), bf16),
            pltpu.VMEM((deep, frames * LANES), bf16),
            pltpu.VMEM((deep, frames * LANES), bf16),
            pltpu.SemaphoreType.DMA,
            pltpu.SemaphoreType.DMA((n,)),
            pltpu.SemaphoreType.DMA((3,)),
            pltpu.SemaphoreType.REGULAR((n,)),
        ],
        compiler_params=pltpu.CompilerParams(
            vmem_limit_bytes=(40 if n <= SMALL else 56) * 1024 * 1024, collective_id=0, has_side_effects=True
        ),
    )(
        stay(jnp.transpose(estimate, (0, 1, 3, 2, 4)).reshape(flat)),
        stay(jnp.transpose(measured, (0, 1, 3, 2, 4)).reshape(flat)),
        stay(sampled_lines),
    )
    return jnp.transpose(out.reshape(parts, coils, rows, frames, readout), (0, 1, 3, 2, 4))


def solution(mesh):
    placed = (
        P(None, None, "grp", "slab", None),
        P(None, None, "grp", "slab", None),
        P("grp", None),
    )
    return jax.shard_map(
        local,
        mesh=mesh,
        in_specs=placed,
        out_specs=P(None, None, "grp", "slab", None),
        check_vma=False,
    )
```

```python
import functools

import jax
import jax.numpy as jnp
from jax import lax
from jax.experimental import pallas as pl
from jax.experimental.pallas import tpu as pltpu
from jax.sharding import PartitionSpec as P

LANES = 128
REACH = 4
SPAN = range(-REACH, REACH + 1)
SMALL = 16


def couplings(frames):
    table = {}
    for s in range(frames):
        for s2 in range(frames):
            for d in range(1 - frames, frames):
                if 0 <= s + d < frames and 0 <= s2 + d < frames:
                    table[s, s2, d] = sum(
                        1
                        for t in range(frames)
                        if 0 <= t + d < frames and abs(s - t) <= 2 and abs(s2 - t) <= 2
                    )
    return {k: v for k, v in table.items() if v}


def halves(x):
    hi = x.astype(jnp.bfloat16)
    return hi, (x - hi.astype(jnp.float32)).astype(jnp.bfloat16)


def dot_nt(a, b):
    return lax.dot_general(a, b, (((1,), (1,)), ((), ())), preferred_element_type=jnp.float32)


def dot_nn(a, b):
    return lax.dot_general(a, b, (((1,), (0,)), ((), ())), preferred_element_type=jnp.float32)


def kernel(
    n, sizes, est_hbm, meas_hbm, picks_hbm, out_ref,
    est, meas, picks, all_ref, even, odd, base, sums, shift, flat, patch, u_hi, u_lo,
    send_sem, recv_sem, in_sem, ready,
):
    parts, frames, coils, rows, readout = sizes
    me = lax.axis_index("slab")
    flip = me >= n // 2
    mine = jnp.where(flip, n - 1 - me, me)
    total = n * rows
    ext = coils * 5
    wide = frames * ext
    bf16 = jnp.bfloat16

    loads = [
        pltpu.make_async_copy(est_hbm, est, in_sem.at[0]),
        pltpu.make_async_copy(meas_hbm, meas, in_sem.at[1]),
        pltpu.make_async_copy(picks_hbm, picks, in_sem.at[2]),
    ]
    for load in loads:
        load.start()

    def greet(j, carry):
        pl.semaphore_signal(pltpu.get_barrier_semaphore(), inc=1, device_id={"slab": j})
        return carry

    lax.fori_loop(me + 1, n, greet, 0)

    def place(line, s, part):
        return pl.ds((part * coils * rows + line) * frames + s, coils, stride=rows * frames)

    loads[0].wait()
    for j in range(rows):
        all_ref[me, j * coils : (j + 1) * coils, :] = jnp.concatenate(
            [est[place(j, s, part), :] for part in range(parts) for s in range(frames)], axis=1
        )
    pl.when(me > 0)(lambda: pl.semaphore_wait(pltpu.get_barrier_semaphore(), me))

    def copy(other, slot):
        return pltpu.make_async_remote_copy(
            src_ref=all_ref.at[slot],
            dst_ref=all_ref.at[slot],
            send_sem=send_sem,
            recv_sem=recv_sem.at[slot],
            device_id={"slab": other},
        )

    def down(j, carry):
        pl.semaphore_signal(ready.at[me], inc=1, device_id={"slab": j})
        copy(j, me).start()
        return carry

    def down_group(t, carry):
        g = me // 4 - t
        return lax.fori_loop(4 * g, jnp.minimum(4 * g + 4, me), down, carry)

    lax.fori_loop(0, jnp.minimum(me, 4), down, 0)
    lax.fori_loop(0, me // 4, down_group, 0)

    def meet(j, carry):
        pl.semaphore_wait(ready.at[j], 1)
        copy(j, me).start()
        return carry

    first_group = me < 4

    def meet_group(t):
        stop = jnp.where(first_group, 4 * t + 4, me + 1)
        lax.fori_loop(jnp.where(first_group, jnp.maximum(me + 1, 4 * t), me + 1), stop, meet, 0)

    lax.fori_loop(me + 1, jnp.where(first_group, me + 1, n), meet, 0)
    meet_group(0)
    meet_group(1)

    def take(k):
        j = jnp.where(flip, n - 1 - k, k)
        pl.when(j != me)(lambda: copy(j, j).wait_recv())

    lane = lax.broadcasted_iota(jnp.int32, (1, LANES), 1)
    slot = lane // readout
    x = lane % readout
    second = slot >= parts
    turn = jnp.where(slot % parts == 0, 1.0, -1.0)
    nothing = jnp.zeros((coils, LANES), jnp.float32)

    def rolled(v, by):
        by = by % LANES
        return pltpu.roll(v, by, 1) if by else v

    def shifts(v):
        return [
            jnp.where((x + d >= 0) & (x + d < readout), rolled(v, -d), 0.0) if d else v
            for d in range(-2, 3)
        ]

    def line_block(line):
        if isinstance(line, int) and not 0 <= line < total:
            return nothing
        dev, j = line // rows, line % rows
        dev = jnp.where(flip, n - 1 - dev, dev)
        j = jnp.where(flip, rows - 1 - j, j)
        return all_ref[dev, pl.ds(pl.multiple_of(j * coils, coils), coils), :]

    order = [(s, e) for s in range(frames) for e in range(5)]

    def reach_of(line):
        inside = [(line - b >= 0) & (line - b < total) for b in range(-2, 3)]
        if isinstance(line, int):
            return float(sum(inside))
        return sum(jnp.where(v, 1.0, 0.0) for v in inside)

    def at_tile(i):
        start = (i // 2 + 2) * LANES
        return pl.ds(start if isinstance(i, int) else pl.multiple_of(start, LANES), LANES)

    pieces_of = len(order)
    row = lax.broadcasted_iota(jnp.int32, (LANES, LANES), 0)
    part_at = slot % parts
    for b, (s, e) in enumerate(order):
        for k, part in enumerate((part_at, 1 - part_at)):
            from_x = x + e - 2
            target = jnp.where(
                (from_x >= 0) & (from_x < readout), (part * frames + s) * readout + from_x, -1
            )
            one = 1.0 if k == 0 else turn
            shift[:, (k * pieces_of + b) * LANES : (k * pieces_of + b + 1) * LANES] = jnp.where(
                row == target, one, 0.0
            ).astype(bf16)

    def absorb(first, count, energy):
        lines = [line_block(first + k) for k in range(count + 1)]
        for k in range(1, count + 1):
            line = first + k
            if not isinstance(line, int) or line < total:
                energy = energy + reach_of(line) * (lines[k] * lines[k])
        raw = jnp.concatenate(lines, axis=0)
        high = raw.astype(bf16).astype(jnp.float32)
        split = jnp.concatenate([high, raw - high], axis=0).astype(bf16)
        g = dot_nn(split, shift[...])

        def piece(k, w, b):
            top = (w * (count + 1) + k) * coils
            return g[top : top + coils, b * LANES : (b + 1) * LANES]

        for step in range(count):
            i = first + step
            is_even = (step + PARITY) % 2 == 0
            tiles = even if is_even else odd
            at = at_tile(i)
            for w in range(2):
                cells = [
                    jnp.where(second, piece(step + 1, w, b), piece(step, w, b))
                    for b in range(pieces_of)
                ]
                tiles[w * wide : (w + 1) * wide, at] = jnp.concatenate(cells, axis=0).astype(bf16)
                if is_even and (not isinstance(i, int) or 0 <= i < total):
                    both = [
                        jnp.where(second, piece(step + 1, w, b), piece(step, w, b))
                        for b in range(pieces_of, 2 * pieces_of)
                    ]
                    stacked = []
                    for s in range(frames):
                        stacked += [cells[order.index((s, e))] for e in range(5)]
                        stacked += [both[order.index((s, e))] for e in range(5)]
                    base[w * 2 * wide : (w + 1) * 2 * wide, at] = jnp.concatenate(
                        stacked, axis=0
                    ).astype(bf16)
        return energy

    gap = jnp.zeros((LANES - 2 * ext, 1), bf16)

    def columns(at, w, count):
        pad = jnp.broadcast_to(gap, (LANES - 2 * ext, count * LANES))
        pieces = []
        for s in range(frames):
            top = w * 2 * wide + s * 2 * ext
            pieces += [base[top : top + 2 * ext, at], pad]
        return jnp.concatenate(pieces, axis=0)

    def lanes_from(tile, count):
        start = (tile + 2) * LANES
        return pl.ds(start if isinstance(tile, int) else pl.multiple_of(start, LANES), count * LANES)

    def stretch(i, w, count):
        tiles = even if i % 2 == 0 else odd
        return tiles[w * wide : (w + 1) * wide, lanes_from(i // 2, count)]

    def product(rows_hi, rows_lo, cols_hi, cols_lo):
        return dot_nt(
            jnp.concatenate([rows_hi, rows_lo, rows_hi], axis=1),
            jnp.concatenate([cols_hi, cols_hi, cols_lo], axis=1),
        )

    def gram(tile, count, fresh=False):
        at = lanes_from(tile, count)

        def moved(w):
            pieces = []
            for dy in range(REACH + 1):
                tiles = even if dy % 2 == 0 else odd
                pieces.append(tiles[w * wide : (w + 1) * wide, lanes_from(tile + dy // 2, count)])
            return jnp.concatenate(pieces, axis=0)

        g = product(moved(0), moved(1), columns(at, 0, count), columns(at, 1, count))
        sums[...] = g if fresh else sums[...] + g

    def edge(i):
        at = lanes_from(i // 2, 1)

        def picked(w):
            zero = jnp.zeros((wide, LANES), bf16)
            return jnp.concatenate(
                [
                    jnp.where(second, zero, stretch(i, w, 1)),
                    jnp.where(second, zero, stretch(i + 1, w, 1)),
                    jnp.where(second, stretch(i - 1, w, 1), zero),
                    jnp.where(second, stretch(i, w, 1), zero),
                ],
                axis=0,
            )

        return product(picked(0), picked(1), columns(at, 0, 1), columns(at, 1, 1))

    ahead = REACH + 1
    members = [(dy, None) for dy in (*range(ahead), *range(-1, -ahead, -1))]
    for i in (0, total - 2):
        members += [(0, i), (1, i), (-1, i + 1), (0, i + 1)]
    depth = len(members) * wide
    deep = -(-depth // LANES) * LANES
    cells_here = rows * readout

    def patches():
        line_at = mine * rows + slot

        def coefficient(dy, q=None):
            count = jnp.zeros((1, LANES), jnp.float32)
            for b in range(max(-2, -2 - dy), min(2, 2 - dy) + 1):
                if q is not None and 0 <= q - b < total:
                    continue
                count = count + jnp.where((line_at - b >= 0) & (line_at - b < total), 1.0, 0.0)
            return count if q is None else -count

        around = []
        for i in range(rows + 2 * REACH):
            line = mine * rows - REACH + i
            block = line_block(jnp.clip(line, 0, total - 1))
            block = jnp.where((line >= 0) & (line < total), block, 0.0)
            around.append([rolled(block, by * readout) for by in range(LANES // readout)])
        for dy in SPAN:
            for part in range(parts):
                cells = []
                for s in range(frames):
                    v = nothing
                    for j in range(rows):
                        seg = part * frames + s
                        v = jnp.where(slot == j, around[dy + REACH + j][(j - seg) % 4], v)
                    cells.append(shifts(v))
                v = jnp.concatenate([cells[s][e] for s, e in order], axis=0)
                for t, (dy2, q) in enumerate(members):
                    if dy2 == dy:
                        factor = float(couplings(frames)[0, 0, 0]) * coefficient(dy, q)
                        flat[part, t * wide : (t + 1) * wide, :] = factor * v
        for part in range(parts):
            for k in range(0, deep, LANES):
                hi, lo = halves(flat[part, k : k + LANES, :].T[:cells_here])
                at = pl.ds(k, LANES)
                patch[pl.ds(part * cells_here, cells_here), at] = hi
                patch[pl.ds((parts + part) * cells_here, cells_here), at] = lo

    table = couplings(frames)
    unit = float(table[0, 0, 0])

    def mixed(u):
        result = []
        for s2 in range(frames):
            pieces = []
            for s in range(frames):
                whole = None
                for d in range(1 - frames, frames):
                    if (s, s2, d) in table:
                        row = (s + d) * ext
                        term = u[row : row + ext, (s2 + d) * LANES : (s2 + d + 1) * LANES]
                        factor = table[s, s2, d] / unit
                        term = term if factor == 1 else factor * term
                        whole = term if whole is None else whole + term
                pieces.append(whole)
            result.append(jnp.concatenate(pieces, axis=0))
        return result

    def settle(t, cells):
        for s2 in range(frames):
            hi, lo = halves(cells[s2])
            at = pl.ds(s2 * LANES, LANES)
            u_hi[t * wide : (t + 1) * wide, at] = hi
            u_lo[t * wide : (t + 1) * wide, at] = lo

    def mirrored(cells):
        pieces = [[], []]
        for s in range(frames):
            spare = jnp.zeros((LANES - wide, LANES), jnp.float32)
            v = jnp.concatenate([cells[s], spare], axis=0).T
            re, im = v[:ext], v[ext : 2 * ext]
            pieces[0].append(jnp.where(lane < ext, re, -rolled(im, ext)))
            pieces[1].append(jnp.where(lane < ext, rolled(re, -ext), -im))
        return [jnp.concatenate(p, axis=0) for p in pieces]

    tall = parts * cells_here

    def filtered(first, count):
        at = pl.ds(first * wide, count * wide)
        both = dot_nn(patch[:, at], u_hi[at, :])
        return both[:tall] + both[tall:] + dot_nn(patch[0:tall, at], u_lo[at, :])

    for i in (total, total + 1, total + 2):
        tiles = even if i % 2 == 0 else odd
        tiles[:, at_tile(i)] = jnp.zeros((2 * wide, LANES), bf16)
    for part in range(parts):
        flat[part, depth:deep, :] = jnp.zeros((deep - depth, LANES), jnp.float32)
    for ref in (u_hi, u_lo):
        ref[depth:deep, :] = jnp.zeros((deep - depth, frames * LANES), bf16)

    group = 4 * rows
    groups = n // 4
    half = group // 2

    def settle_edge(first, i):
        g = edge(i)
        for k in range(4):
            settle(first + k, mixed(g[k * wide : (k + 1) * wide]))

    for load in loads[1:]:
        load.wait()
    energy = nothing
    early = []
    PARITY = 1
    if n <= SMALL:
        for t in range(2, groups - 1):
            meet_group(t)
        seen, done = 0, 0
        for stop in (n // 4, n // 2, n - 2, n):
            for k in range(seen, stop):
                take(k)
            if stop == n // 2:
                meet_group(groups - 1)
            first = seen * rows - 1
            PARITY = first % 2
            energy = absorb(first, (stop - seen) * rows + (stop == n), energy)
            if stop in (n // 2, n - 2, n):
                reached = total if stop == n else (stop * rows - REACH) // 4 * 4
                gram(done // 2, (reached - done) // 2, fresh=done == 0)
                done = reached
            if seen == 0:
                settle_edge(len(SPAN), 0)
            if stop == n - 2:
                patches()
                early.append(filtered(len(SPAN), 4))
            seen = stop
    else:
        lax.fori_loop(2, groups, lambda t, c: (meet_group(t), c)[1], 0)

        def pairs(t):
            for k in range(4):
                take(4 * t + k)

        pairs(0)
        energy = absorb(-1, group, energy)
        gram(0, (group - REACH) // 2, fresh=True)
        settle_edge(len(SPAN), 0)

        def step(t, energy):
            pairs(t)
            energy = absorb(group * t - 1, group, energy)
            gram((group * t - REACH) // 2, group // 2)
            return energy

        energy = lax.fori_loop(1, groups - 1, step, energy)
        pairs(groups - 1)
        first = group * (groups - 1)
        energy = absorb(first - 1, group + 1, energy)
        gram((first - REACH) // 2, (group + REACH) // 2)
        patches()

    for t in (*range(1, ahead), 0):
        cells = mixed(sums[t * wide : (t + 1) * wide, :])
        settle(t, cells)
        if t:
            settle(REACH + t, mirrored(cells))
    settle_edge(len(SPAN) + 4, total - 2)

    across = sum(jnp.where((x - d >= 0) & (x - d < readout), 1.0, 0.0) for d in range(-2, 3))
    frame = slot % frames
    for s in range(frames):
        reach = sum(1.0 for t in range(frames) if abs(s - t) <= 2)
        across = jnp.where(frame == s, across * reach, across)
    energy = jnp.sum(energy * across, axis=0, keepdims=True)
    scale = jnp.sum(energy, axis=1, keepdims=True) / (125 * coils) + 1e-06
    factor = 1.0 / (125.0 * scale)

    y = filtered(0, len(SPAN)) + filtered(len(SPAN) + 4, 4)
    for part in early or [filtered(len(SPAN), 4)]:
        y = y + part

    chosen = picks[...]
    spare = jnp.zeros((LANES - cells_here, LANES), jnp.float32)
    for s in range(frames):
        turned = []
        for part in range(parts):
            v = y[part * cells_here : (part + 1) * cells_here, s * LANES : (s + 1) * LANES]
            turned.append((jnp.concatenate([v, spare], axis=0) if cells_here < LANES else v).T)
        for part in range(parts):
            folded = nothing
            for e in range(5):
                plain = slice(e * coils, (e + 1) * coils)
                cross = slice(ext + e * coils, ext + (e + 1) * coils)
                if part == 0:
                    v = turned[0][plain] - turned[1][cross]
                else:
                    v = turned[0][cross] + turned[1][plain]
                d = e - 2
                v = jnp.where((x - d >= 0) & (x - d < readout), rolled(v, d), 0.0) if d else v
                folded = folded + v
            folded = folded * factor
            for j in range(rows):
                hit = jnp.where(chosen[s : s + 1, :] == me * rows + j, 1.0, 0.0)
                hit = jnp.max(hit, axis=1, keepdims=True)
                at = place(j, s, part)
                there = jnp.where(
                    flip, rolled(folded, (j + 1 - rows) * readout), rolled(folded, -j * readout)
                )
                out_ref[at, :] = jnp.where(hit > 0.5, meas[at, :], there[:, :readout])

    others = all_ref.at[pl.ds(0, n - 1)]
    pltpu.make_async_remote_copy(
        src_ref=others,
        dst_ref=others,
        send_sem=send_sem,
        recv_sem=recv_sem.at[me],
        device_id={"slab": lax.rem(me + 1, n)},
    ).wait_send()


def local(estimate, measured, sampled_lines):
    parts, coils, frames, rows, readout = estimate.shape
    n = lax.axis_size("slab")
    assert parts * frames * readout == LANES and frames == 2 and coils == 8
    assert rows * readout <= LANES and n % 4 == 0 and n >= 8 and 4 * rows >= 3 * REACH
    flat = (parts * coils * rows * frames, readout)
    total = n * rows
    wide = frames * 5 * coils
    span = (total // 2 + 4) * LANES
    deep = -(-(len(SPAN) + 8) * wide // LANES) * LANES
    cells = rows * readout
    bf16 = jnp.bfloat16
    stay = functools.partial(pltpu.with_memory_space_constraint, memory_space=pltpu.HBM)
    out = pl.pallas_call(
        functools.partial(kernel, n, (parts, frames, coils, rows, readout)),
        out_shape=jax.ShapeDtypeStruct(flat, jnp.float32),
        in_specs=[pl.BlockSpec(memory_space=pltpu.HBM)] * 3,
        out_specs=pl.BlockSpec(memory_space=pltpu.VMEM),
        scratch_shapes=[
            pltpu.VMEM(flat, jnp.float32),
            pltpu.VMEM(flat, jnp.float32),
            pltpu.VMEM(sampled_lines.shape, jnp.int32),
            pltpu.VMEM((n, rows * coils, LANES), jnp.float32),
            pltpu.VMEM((2 * wide, span), bf16),
            pltpu.VMEM((2 * wide, span), bf16),
            pltpu.VMEM((4 * wide, span), bf16),
            pltpu.VMEM(((REACH + 1) * wide, frames * LANES), jnp.float32),
            pltpu.VMEM((LANES, 2 * frames * 5 * LANES), bf16),
            pltpu.VMEM((parts, deep, LANES), jnp.float32),
            pltpu.VMEM((2 * parts * cells, deep), bf16),
            pltpu.VMEM((deep, frames * LANES), bf16),
            pltpu.VMEM((deep, frames * LANES), bf16),
            pltpu.SemaphoreType.DMA,
            pltpu.SemaphoreType.DMA((n,)),
            pltpu.SemaphoreType.DMA((3,)),
            pltpu.SemaphoreType.REGULAR((n,)),
        ],
        compiler_params=pltpu.CompilerParams(
            vmem_limit_bytes=(40 if n <= SMALL else 56) * 1024 * 1024, collective_id=0, has_side_effects=True
        ),
    )(
        stay(jnp.transpose(estimate, (0, 1, 3, 2, 4)).reshape(flat)),
        stay(jnp.transpose(measured, (0, 1, 3, 2, 4)).reshape(flat)),
        stay(sampled_lines),
    )
    return jnp.transpose(out.reshape(parts, coils, rows, frames, readout), (0, 1, 3, 2, 4))


def solution(mesh):
    placed = (
        P(None, None, "grp", "slab", None),
        P(None, None, "grp", "slab", None),
        P("grp", None),
    )
    return jax.shard_map(
        local,
        mesh=mesh,
        in_specs=placed,
        out_specs=P(None, None, "grp", "slab", None),
        check_vma=False,
    )
```

```python
import functools

import jax
import jax.numpy as jnp
from jax import lax
from jax.experimental import pallas as pl
from jax.experimental.pallas import tpu as pltpu
from jax.sharding import PartitionSpec as P

LANES = 128
REACH = 4
SPAN = range(-REACH, REACH + 1)
SMALL = 16


def couplings(frames):
    table = {}
    for s in range(frames):
        for s2 in range(frames):
            for d in range(1 - frames, frames):
                if 0 <= s + d < frames and 0 <= s2 + d < frames:
                    table[s, s2, d] = sum(
                        1
                        for t in range(frames)
                        if 0 <= t + d < frames and abs(s - t) <= 2 and abs(s2 - t) <= 2
                    )
    return {k: v for k, v in table.items() if v}


def halves(x):
    hi = x.astype(jnp.bfloat16)
    return hi, (x - hi.astype(jnp.float32)).astype(jnp.bfloat16)


def dot_nt(a, b):
    return lax.dot_general(a, b, (((1,), (1,)), ((), ())), preferred_element_type=jnp.float32)


def dot_nn(a, b):
    return lax.dot_general(a, b, (((1,), (0,)), ((), ())), preferred_element_type=jnp.float32)


def kernel(
    n, sizes, est_hbm, meas_hbm, picks_hbm, out_ref,
    est, meas, picks, all_ref, even, odd, base, sums, shift, flat, patch, u_hi, u_lo,
    send_sem, recv_sem, in_sem, ready,
):
    parts, frames, coils, rows, readout = sizes
    me = lax.axis_index("slab")
    flip = me >= n // 2
    mine = jnp.where(flip, n - 1 - me, me)
    total = n * rows
    ext = coils * 5
    wide = frames * ext
    bf16 = jnp.bfloat16

    loads = [
        pltpu.make_async_copy(est_hbm, est, in_sem.at[0]),
        pltpu.make_async_copy(meas_hbm, meas, in_sem.at[1]),
        pltpu.make_async_copy(picks_hbm, picks, in_sem.at[2]),
    ]
    for load in loads:
        load.start()

    def greet(j, carry):
        pl.semaphore_signal(pltpu.get_barrier_semaphore(), inc=1, device_id={"slab": j})
        return carry

    lax.fori_loop(me + 1, n, greet, 0)

    def place(line, s, part):
        return pl.ds((part * coils * rows + line) * frames + s, coils, stride=rows * frames)

    loads[0].wait()
    for j in range(rows):
        all_ref[me, j * coils : (j + 1) * coils, :] = jnp.concatenate(
            [est[place(j, s, part), :] for part in range(parts) for s in range(frames)], axis=1
        )
    pl.when(me > 0)(lambda: pl.semaphore_wait(pltpu.get_barrier_semaphore(), me))

    def copy(other, slot):
        return pltpu.make_async_remote_copy(
            src_ref=all_ref.at[slot],
            dst_ref=all_ref.at[slot],
            send_sem=send_sem,
            recv_sem=recv_sem.at[slot],
            device_id={"slab": other},
        )

    def down(j, carry):
        pl.semaphore_signal(ready.at[me], inc=1, device_id={"slab": j})
        copy(j, me).start()
        return carry

    def down_group(t, carry):
        g = me // 4 - t
        return lax.fori_loop(4 * g, jnp.minimum(4 * g + 4, me), down, carry)

    lax.fori_loop(0, jnp.minimum(me, 4), down, 0)
    lax.fori_loop(0, me // 4, down_group, 0)

    def meet(j, carry):
        pl.semaphore_wait(ready.at[j], 1)
        copy(j, me).start()
        return carry

    first_group = me < 4

    def meet_group(t):
        stop = jnp.where(first_group, 4 * t + 4, me + 1)
        lax.fori_loop(jnp.where(first_group, jnp.maximum(me + 1, 4 * t), me + 1), stop, meet, 0)

    lax.fori_loop(me + 1, jnp.where(first_group, me + 1, n), meet, 0)
    meet_group(0)
    meet_group(1)

    def take(k):
        j = jnp.where(flip, n - 1 - k, k)
        pl.when(j != me)(lambda: copy(j, j).wait_recv())

    lane = lax.broadcasted_iota(jnp.int32, (1, LANES), 1)
    slot = lane // readout
    x = lane % readout
    second = slot >= parts
    turn = jnp.where(slot % parts == 0, 1.0, -1.0)
    nothing = jnp.zeros((coils, LANES), jnp.float32)

    def rolled(v, by):
        by = by % LANES
        return pltpu.roll(v, by, 1) if by else v

    def shifts(v):
        return [
            jnp.where((x + d >= 0) & (x + d < readout), rolled(v, -d), 0.0) if d else v
            for d in range(-2, 3)
        ]

    def line_block(line):
        if isinstance(line, int) and not 0 <= line < total:
            return nothing
        dev, j = line // rows, line % rows
        dev = jnp.where(flip, n - 1 - dev, dev)
        j = jnp.where(flip, rows - 1 - j, j)
        return all_ref[dev, pl.ds(pl.multiple_of(j * coils, coils), coils), :]

    order = [(s, e) for s in range(frames) for e in range(5)]

    def reach_of(line):
        inside = [(line - b >= 0) & (line - b < total) for b in range(-2, 3)]
        if isinstance(line, int):
            return float(sum(inside))
        return sum(jnp.where(v, 1.0, 0.0) for v in inside)

    def at_tile(i):
        start = (i // 2 + 2) * LANES
        return pl.ds(start if isinstance(i, int) else pl.multiple_of(start, LANES), LANES)

    pieces_of = len(order)
    row = lax.broadcasted_iota(jnp.int32, (LANES, LANES), 0)
    part_at = slot % parts
    for b, (s, e) in enumerate(order):
        for k, part in enumerate((part_at, 1 - part_at)):
            from_x = x + e - 2
            target = jnp.where(
                (from_x >= 0) & (from_x < readout), (part * frames + s) * readout + from_x, -1
            )
            one = 1.0 if k == 0 else turn
            shift[:, (k * pieces_of + b) * LANES : (k * pieces_of + b + 1) * LANES] = jnp.where(
                row == target, one, 0.0
            ).astype(bf16)

    def absorb(first, count, energy):
        lines = [line_block(first + k) for k in range(count + 1)]
        for k in range(1, count + 1):
            line = first + k
            if not isinstance(line, int) or line < total:
                energy = energy + reach_of(line) * (lines[k] * lines[k])
        raw = jnp.concatenate(lines, axis=0)
        high = raw.astype(bf16).astype(jnp.float32)
        split = jnp.concatenate([high, raw - high], axis=0).astype(bf16)
        g = dot_nn(split, shift[...])

        def piece(k, w, b):
            top = (w * (count + 1) + k) * coils
            return g[top : top + coils, b * LANES : (b + 1) * LANES]

        for step in range(count):
            i = first + step
            is_even = (step + PARITY) % 2 == 0
            tiles = even if is_even else odd
            at = at_tile(i)
            for w in range(2):
                cells = [
                    jnp.where(second, piece(step + 1, w, b), piece(step, w, b))
                    for b in range(pieces_of)
                ]
                tiles[w * wide : (w + 1) * wide, at] = jnp.concatenate(cells, axis=0).astype(bf16)
                if is_even and (not isinstance(i, int) or 0 <= i < total):
                    both = [
                        jnp.where(second, piece(step + 1, w, b), piece(step, w, b))
                        for b in range(pieces_of, 2 * pieces_of)
                    ]
                    stacked = []
                    for s in range(frames):
                        stacked += [cells[order.index((s, e))] for e in range(5)]
                        stacked += [both[order.index((s, e))] for e in range(5)]
                    base[w * 2 * wide : (w + 1) * 2 * wide, at] = jnp.concatenate(
                        stacked, axis=0
                    ).astype(bf16)
        return energy

    gap = jnp.zeros((LANES - 2 * ext, 1), bf16)

    def columns(at, w, count):
        pad = jnp.broadcast_to(gap, (LANES - 2 * ext, count * LANES))
        pieces = []
        for s in range(frames):
            top = w * 2 * wide + s * 2 * ext
            pieces += [base[top : top + 2 * ext, at], pad]
        return jnp.concatenate(pieces, axis=0)

    def lanes_from(tile, count):
        start = (tile + 2) * LANES
        return pl.ds(start if isinstance(tile, int) else pl.multiple_of(start, LANES), count * LANES)

    def stretch(i, w, count):
        tiles = even if i % 2 == 0 else odd
        return tiles[w * wide : (w + 1) * wide, lanes_from(i // 2, count)]

    def product(rows_hi, rows_lo, cols_hi, cols_lo):
        return dot_nt(
            jnp.concatenate([rows_hi, rows_lo, rows_hi], axis=1),
            jnp.concatenate([cols_hi, cols_hi, cols_lo], axis=1),
        )

    def gram(tile, count, fresh=False):
        at = lanes_from(tile, count)

        def moved(w):
            pieces = []
            for dy in range(REACH + 1):
                tiles = even if dy % 2 == 0 else odd
                pieces.append(tiles[w * wide : (w + 1) * wide, lanes_from(tile + dy // 2, count)])
            return jnp.concatenate(pieces, axis=0)

        g = product(moved(0), moved(1), columns(at, 0, count), columns(at, 1, count))
        sums[...] = g if fresh else sums[...] + g

    def edge(i):
        at = lanes_from(i // 2, 1)

        def picked(w):
            zero = jnp.zeros((wide, LANES), bf16)
            return jnp.concatenate(
                [
                    jnp.where(second, zero, stretch(i, w, 1)),
                    jnp.where(second, zero, stretch(i + 1, w, 1)),
                    jnp.where(second, stretch(i - 1, w, 1), zero),
                    jnp.where(second, stretch(i, w, 1), zero),
                ],
                axis=0,
            )

        return product(picked(0), picked(1), columns(at, 0, 1), columns(at, 1, 1))

    ahead = REACH + 1
    members = [(dy, None) for dy in (*range(ahead), *range(-1, -ahead, -1))]
    for i in (0, total - 2):
        members += [(0, i), (1, i), (-1, i + 1), (0, i + 1)]
    depth = len(members) * wide
    deep = -(-depth // LANES) * LANES
    cells_here = rows * readout

    def patches():
        line_at = mine * rows + slot

        def coefficient(dy, q=None):
            count = jnp.zeros((1, LANES), jnp.float32)
            for b in range(max(-2, -2 - dy), min(2, 2 - dy) + 1):
                if q is not None and 0 <= q - b < total:
                    continue
                count = count + jnp.where((line_at - b >= 0) & (line_at - b < total), 1.0, 0.0)
            return count if q is None else -count

        around = []
        for i in range(rows + 2 * REACH):
            line = mine * rows - REACH + i
            block = line_block(jnp.clip(line, 0, total - 1))
            block = jnp.where((line >= 0) & (line < total), block, 0.0)
            around.append([rolled(block, by * readout) for by in range(LANES // readout)])
        for dy in SPAN:
            for part in range(parts):
                cells = []
                for s in range(frames):
                    v = nothing
                    for j in range(rows):
                        seg = part * frames + s
                        v = jnp.where(slot == j, around[dy + REACH + j][(j - seg) % 4], v)
                    cells.append(shifts(v))
                v = jnp.concatenate([cells[s][e] for s, e in order], axis=0)
                for t, (dy2, q) in enumerate(members):
                    if dy2 == dy:
                        factor = float(couplings(frames)[0, 0, 0]) * coefficient(dy, q)
                        flat[part, t * wide : (t + 1) * wide, :] = factor * v
        for part in range(parts):
            for k in range(0, deep, LANES):
                hi, lo = halves(flat[part, k : k + LANES, :].T[:cells_here])
                at = pl.ds(k, LANES)
                patch[pl.ds(part * cells_here, cells_here), at] = hi
                patch[pl.ds((parts + part) * cells_here, cells_here), at] = lo

    table = couplings(frames)
    unit = float(table[0, 0, 0])

    def mixed(u):
        result = []
        for s2 in range(frames):
            pieces = []
            for s in range(frames):
                whole = None
                for d in range(1 - frames, frames):
                    if (s, s2, d) in table:
                        row = (s + d) * ext
                        term = u[row : row + ext, (s2 + d) * LANES : (s2 + d + 1) * LANES]
                        factor = table[s, s2, d] / unit
                        term = term if factor == 1 else factor * term
                        whole = term if whole is None else whole + term
                pieces.append(whole)
            result.append(jnp.concatenate(pieces, axis=0))
        return result

    def settle(t, cells):
        for s2 in range(frames):
            hi, lo = halves(cells[s2])
            at = pl.ds(s2 * LANES, LANES)
            u_hi[t * wide : (t + 1) * wide, at] = hi
            u_lo[t * wide : (t + 1) * wide, at] = lo

    def mirrored(cells):
        pieces = [[], []]
        for s in range(frames):
            spare = jnp.zeros((LANES - wide, LANES), jnp.float32)
            v = jnp.concatenate([cells[s], spare], axis=0).T
            re, im = v[:ext], v[ext : 2 * ext]
            pieces[0].append(jnp.where(lane < ext, re, -rolled(im, ext)))
            pieces[1].append(jnp.where(lane < ext, rolled(re, -ext), -im))
        return [jnp.concatenate(p, axis=0) for p in pieces]

    tall = parts * cells_here

    def filtered(first, count):
        at = pl.ds(first * wide, count * wide)
        both = dot_nn(patch[:, at], u_hi[at, :])
        return both[:tall] + both[tall:] + dot_nn(patch[0:tall, at], u_lo[at, :])

    for i in (total, total + 1, total + 2):
        tiles = even if i % 2 == 0 else odd
        tiles[:, at_tile(i)] = jnp.zeros((2 * wide, LANES), bf16)
    for part in range(parts):
        flat[part, depth:deep, :] = jnp.zeros((deep - depth, LANES), jnp.float32)
    for ref in (u_hi, u_lo):
        ref[depth:deep, :] = jnp.zeros((deep - depth, frames * LANES), bf16)

    group = 4 * rows
    groups = n // 4
    half = group // 2

    def settle_edge(first, i):
        g = edge(i)
        for k in range(4):
            settle(first + k, mixed(g[k * wide : (k + 1) * wide]))

    for load in loads[1:]:
        load.wait()
    chosen = picks[...]
    hits = {}
    for s in range(frames):
        for j in range(rows):
            hit = jnp.where(chosen[s : s + 1, :] == me * rows + j, 1.0, 0.0)
            hits[s, j] = jnp.max(hit, axis=1, keepdims=True)
    energy = nothing
    early = []
    PARITY = 1
    if n <= SMALL:
        for t in range(2, groups - 1):
            meet_group(t)
        seen, done = 0, 0
        for stop in (n // 4, n // 2, n - 2, n):
            for k in range(seen, stop):
                take(k)
            first = seen * rows - 1
            PARITY = first % 2
            energy = absorb(first, (stop - seen) * rows + (stop == n), energy)
            if stop == n // 2:
                meet_group(groups - 1)
            if stop in (n // 2, n - 2, n):
                reached = total if stop == n else (stop * rows - REACH) // 4 * 4
                gram(done // 2, (reached - done) // 2, fresh=done == 0)
                done = reached
            if seen == 0:
                settle_edge(len(SPAN), 0)
            if stop == n - 2:
                patches()
                early.append(filtered(len(SPAN), 4))
            seen = stop
    else:
        lax.fori_loop(2, groups, lambda t, c: (meet_group(t), c)[1], 0)

        def pairs(t):
            for k in range(4):
                take(4 * t + k)

        pairs(0)
        energy = absorb(-1, group, energy)
        gram(0, (group - REACH) // 2, fresh=True)
        settle_edge(len(SPAN), 0)

        def step(t, energy):
            pairs(t)
            energy = absorb(group * t - 1, group, energy)
            gram((group * t - REACH) // 2, group // 2)
            return energy

        energy = lax.fori_loop(1, groups - 1, step, energy)
        pairs(groups - 1)
        first = group * (groups - 1)
        energy = absorb(first - 1, group + 1, energy)
        gram((first - REACH) // 2, (group + REACH) // 2)
        patches()

    for t in (*range(1, ahead), 0):
        cells = mixed(sums[t * wide : (t + 1) * wide, :])
        settle(t, cells)
        if t:
            settle(REACH + t, mirrored(cells))
    settle_edge(len(SPAN) + 4, total - 2)

    across = sum(jnp.where((x - d >= 0) & (x - d < readout), 1.0, 0.0) for d in range(-2, 3))
    frame = slot % frames
    for s in range(frames):
        reach = sum(1.0 for t in range(frames) if abs(s - t) <= 2)
        across = jnp.where(frame == s, across * reach, across)
    energy = jnp.sum(energy * across, axis=0, keepdims=True)
    scale = jnp.sum(energy, axis=1, keepdims=True) / (125 * coils) + 1e-06
    factor = 1.0 / (125.0 * scale)

    y = filtered(0, len(SPAN)) + filtered(len(SPAN) + 4, 4)
    for part in early or [filtered(len(SPAN), 4)]:
        y = y + part

    spare = jnp.zeros((LANES - cells_here, LANES), jnp.float32)
    for s in range(frames):
        turned = []
        for part in range(parts):
            v = y[part * cells_here : (part + 1) * cells_here, s * LANES : (s + 1) * LANES]
            turned.append((jnp.concatenate([v, spare], axis=0) if cells_here < LANES else v).T)
        for part in range(parts):
            folded = nothing
            for e in range(5):
                plain = slice(e * coils, (e + 1) * coils)
                cross = slice(ext + e * coils, ext + (e + 1) * coils)
                if part == 0:
                    v = turned[0][plain] - turned[1][cross]
                else:
                    v = turned[0][cross] + turned[1][plain]
                d = e - 2
                v = jnp.where((x - d >= 0) & (x - d < readout), rolled(v, d), 0.0) if d else v
                folded = folded + v
            folded = folded * factor
            for j in range(rows):
                hit = hits[s, j]
                at = place(j, s, part)
                there = jnp.where(
                    flip, rolled(folded, (j + 1 - rows) * readout), rolled(folded, -j * readout)
                )
                out_ref[at, :] = jnp.where(hit > 0.5, meas[at, :], there[:, :readout])

    others = all_ref.at[pl.ds(0, n - 1)]
    pltpu.make_async_remote_copy(
        src_ref=others,
        dst_ref=others,
        send_sem=send_sem,
        recv_sem=recv_sem.at[me],
        device_id={"slab": lax.rem(me + 1, n)},
    ).wait_send()


def local(estimate, measured, sampled_lines):
    parts, coils, frames, rows, readout = estimate.shape
    n = lax.axis_size("slab")
    assert parts * frames * readout == LANES and frames == 2 and coils == 8
    assert rows * readout <= LANES and n % 4 == 0 and n >= 8 and 4 * rows >= 3 * REACH
    flat = (parts * coils * rows * frames, readout)
    total = n * rows
    wide = frames * 5 * coils
    span = (total // 2 + 4) * LANES
    deep = -(-(len(SPAN) + 8) * wide // LANES) * LANES
    cells = rows * readout
    bf16 = jnp.bfloat16
    stay = functools.partial(pltpu.with_memory_space_constraint, memory_space=pltpu.HBM)
    out = pl.pallas_call(
        functools.partial(kernel, n, (parts, frames, coils, rows, readout)),
        out_shape=jax.ShapeDtypeStruct(flat, jnp.float32),
        in_specs=[pl.BlockSpec(memory_space=pltpu.HBM)] * 3,
        out_specs=pl.BlockSpec(memory_space=pltpu.VMEM),
        scratch_shapes=[
            pltpu.VMEM(flat, jnp.float32),
            pltpu.VMEM(flat, jnp.float32),
            pltpu.VMEM(sampled_lines.shape, jnp.int32),
            pltpu.VMEM((n, rows * coils, LANES), jnp.float32),
            pltpu.VMEM((2 * wide, span), bf16),
            pltpu.VMEM((2 * wide, span), bf16),
            pltpu.VMEM((4 * wide, span), bf16),
            pltpu.VMEM(((REACH + 1) * wide, frames * LANES), jnp.float32),
            pltpu.VMEM((LANES, 2 * frames * 5 * LANES), bf16),
            pltpu.VMEM((parts, deep, LANES), jnp.float32),
            pltpu.VMEM((2 * parts * cells, deep), bf16),
            pltpu.VMEM((deep, frames * LANES), bf16),
            pltpu.VMEM((deep, frames * LANES), bf16),
            pltpu.SemaphoreType.DMA,
            pltpu.SemaphoreType.DMA((n,)),
            pltpu.SemaphoreType.DMA((3,)),
            pltpu.SemaphoreType.REGULAR((n,)),
        ],
        compiler_params=pltpu.CompilerParams(
            vmem_limit_bytes=(40 if n <= SMALL else 56) * 1024 * 1024, collective_id=0, has_side_effects=True
        ),
    )(
        stay(jnp.transpose(estimate, (0, 1, 3, 2, 4)).reshape(flat)),
        stay(jnp.transpose(measured, (0, 1, 3, 2, 4)).reshape(flat)),
        stay(sampled_lines),
    )
    return jnp.transpose(out.reshape(parts, coils, rows, frames, readout), (0, 1, 3, 2, 4))


def solution(mesh):
    placed = (
        P(None, None, "grp", "slab", None),
        P(None, None, "grp", "slab", None),
        P("grp", None),
    )
    return jax.shard_map(
        local,
        mesh=mesh,
        in_specs=placed,
        out_specs=P(None, None, "grp", "slab", None),
        check_vma=False,
    )
```
